128 devices in a mesh: gx: 16 (over x, y_hi, core), gy: 8 (over y_lo, z).
Axes of the slice: x: 4, y: 4 (y_hi: 2, y_lo: 2; y = y_hi * 2 + y_lo), z: 4, core: 2. Of those that a mesh axis runs over, the one named last changes fastest.
Arguments:
- features: bfloat16 [16, 8, 2048, 256], P('gx', 'gy'), may hold values from -6 to 6
- neighbours: int32 [16, 8, 27, 2048], P('gx', 'gy'), may hold values from 0 to 2048, as said below
- counts: int32 [16, 8], P('gx', 'gy'), may hold values from 1024 to 2048, as said below
- block_dest: int32 [16, 8, 128], P('gx', 'gy'), may hold values from 0 to 16383, as said below
- conv_weight: bfloat16 [27, 256, 256], replicated, may hold values from -0.078125 to 0.078125
- cpe_weight: bfloat16 [256, 256], replicated, may hold values from -0.375 to 0.375
- cpe_gain: float32 [256], replicated, may hold values from 0.25 to 1.75
- norm1_gain: float32 [256], replicated, may hold values from 0.25 to 1.75
- qkv_weight: bfloat16 [256, 768], replicated
- proj_weight: bfloat16 [256, 256], replicated, may hold values from -0.375 to 0.375
- norm2_gain: float32 [256], replicated, may hold values from 0.25 to 1.75
- fc1_weight: bfloat16 [256, 1024], replicated, may hold values from -0.375 to 0.375
- fc2_weight: bfloat16 [1024, 256], replicated, may hold values from -0.1875 to 0.1875
Outputs:
- block_out: bfloat16 [16, 8, 2048, 256], P('gx', 'gy')
The draws below stay inside these ranges and needn't reach their ends.
Inputs may be any that keep to these rules, and one draw needn't show every extreme that they name: `neighbours`: tap 13 of every row is the row itself; the value 2048 marks a missing neighbour; other values are rows of the same device. `counts`: every device has at least 1024 live rows; some device has exactly 2048 and some exactly 1024; the offset of every device but the first is not a multiple of 1024. `block_dest`: every value appears exactly once; the blocks of one device go to different devices.
All inputs are finite; a program needn't handle non-finite values.
Results may differ from the reference program's by a relative error of at most 0.0095.
The reference program's roundings to bfloat16 on the way count: a program that leaves them out, or rounds other values in their place, can miss the bound.
Values may be sent and summed in bfloat16 or wider, within the bound.
A program may use at most 448 MiB of HBM per device.

```python
import jax
import jax.numpy as jnp
from jax import lax

C = 256
HEADS = 16
FFN = 1024
PATCH = 1024
ROWS = 2048
NB = 128
BLOCK = 16
HEAD_DIM = 16
GRID_X = 16
GRID_Y = 8


def draw_neighbours(key, part):
    key_shift, key_keep = jax.random.split(key)
    grid_shape = (GRID_X, GRID_Y, 27, ROWS)
    row_index = jnp.arange(ROWS, dtype=jnp.int32)
    shifted = row_index + jax.random.randint(key_shift, grid_shape, -48, 49)
    nearby = jnp.clip(shifted, 0, ROWS - 1)
    present = jax.random.randint(key_keep, grid_shape, 0, 2) == 1
    chosen = jnp.where(present, nearby, ROWS)
    centre_tap = (jnp.arange(27) == 13)[None, None, :, None]
    return jnp.where(centre_tap, row_index, chosen).astype(jnp.int32)


def draw_counts(key, part):
    devices = GRID_X * GRID_Y
    key_resid, key_high, key_step, key_patches, key_last = jax.random.split(key, 5)
    high_spot = jax.random.randint(key_high, (), 1, devices)
    low_spot = 1 + (high_spot - 1 + 1 + jax.random.randint(key_step, (), 0, devices - 2)) % (devices - 1)
    device_index = jnp.arange(devices, dtype=jnp.int32)
    is_spot = (device_index == high_spot) | (device_index == low_spot)
    fresh = jax.random.randint(key_resid, (devices,), 1, PATCH)

    def next_resid(previous, pair_in):
        fresh_value, prev_spot = pair_in
        value = jnp.where(prev_spot, previous, fresh_value).astype(jnp.int32)
        return (value, value)
    prev_spots = jnp.concatenate([jnp.zeros((1,), bool), is_spot[:-1]])
    _, resid_rest = lax.scan(next_resid, jnp.int32(0), (fresh[1:], prev_spots[1:]))
    resid = jnp.concatenate([jnp.zeros((1,), jnp.int32), resid_rest])
    following = jnp.concatenate([resid[1:], jnp.zeros((1,), jnp.int32)])
    remainder = (following - resid) % PATCH
    last_rem = jax.random.randint(key_last, (), 0, PATCH)
    remainder = jnp.where(device_index == devices - 1, last_rem, remainder)
    remainder = jnp.where(is_spot, 0, remainder)
    full_patches = ROWS // PATCH
    top_patches = jnp.where(remainder > 0, full_patches - 1, full_patches)
    picked = jax.random.randint(key_patches, (devices,), 0, 1 << 20) % top_patches + 1
    drawn = picked * PATCH + remainder
    drawn = jnp.where(device_index == high_spot, ROWS, drawn)
    drawn = jnp.where(device_index == low_spot, PATCH, drawn)
    return drawn.reshape(GRID_X, GRID_Y).astype(jnp.int32)


def draw_block_dest(key, part):
    devices = GRID_X * GRID_Y
    key_order, key_offsets, key_shift = jax.random.split(key, 3)
    order = jax.random.permutation(key_order, devices)
    inverse = jnp.argsort(order)
    offsets = jax.random.permutation(key_offsets, devices)[:NB]
    shifts = jax.random.randint(key_shift, (devices,), 0, NB)
    source_rank = inverse[jnp.arange(devices)]
    target = order[(source_rank[:, None] + offsets[None, :]) % devices]
    slot_index = (jnp.arange(NB)[None, :] + shifts[target]) % NB
    return (target * NB + slot_index).reshape(GRID_X, GRID_Y, NB).astype(jnp.int32)


def draw_qkv_weight(key, part):
    base = jax.random.normal(key, (C, 3 * C), jnp.float32) * C ** (-0.5)
    return base.astype(jnp.bfloat16)


def levels(rng, extent, cuts, smallest, largest):
    gain, own = 1.0, jax.random.fold_in(rng, 6)
    for dim, parts in cuts:
        draws = jnp.exp(jax.random.uniform(jax.random.fold_in(own, dim), (parts,), jnp.float32, smallest / len(cuts), largest / len(cuts)))
        gain = gain * jnp.repeat(draws, extent[dim] // parts).reshape([-1 if axis == dim else 1 for axis in range(len(extent))])
    return gain


def normal_values(key, extent, width, reach, cuts=(), kind=jnp.bfloat16):
    entries = width * jax.random.normal(key, extent, jnp.float32)
    if cuts:
        entries = entries * levels(key, extent, cuts, -0.22, 0.18)
    return jnp.clip(entries, -reach, reach).astype(kind)


def setup_inputs(seed: int = 0) -> dict:
    key_list = jax.random.split(jax.random.key(seed), 14)
    features = normal_values(key_list[0], (GRID_X, GRID_Y, ROWS, C), 1.0, 6.0, ((0, 16), (1, 8)))
    neighbours = draw_neighbours(jax.random.fold_in(key_list[13], 71), 0)
    counts = draw_counts(jax.random.fold_in(key_list[13], 71), 0)
    block_dest = draw_block_dest(jax.random.fold_in(key_list[13], 71), 0)
    conv_weight = normal_values(key_list[4], (27, C, C), (27 * C) ** -0.5, 0.078125)
    cpe_weight = normal_values(key_list[5], (C, C), C ** -0.5, 0.375)
    cpe_gain = jnp.clip(1.0 + 0.15 * jax.random.normal(key_list[6], (C,), jnp.float32), 0.25, 1.75)
    norm1_gain = jnp.clip(1.0 + 0.15 * jax.random.normal(key_list[7], (C,), jnp.float32), 0.25, 1.75)
    qkv_weight = draw_qkv_weight(jax.random.fold_in(key_list[13], 71), 0)
    proj_weight = normal_values(key_list[9], (C, C), C ** -0.5, 0.375)
    norm2_gain = jnp.clip(1.0 + 0.15 * jax.random.normal(key_list[10], (C,), jnp.float32), 0.25, 1.75)
    fc1_weight = normal_values(key_list[11], (C, FFN), C ** -0.5, 0.375)
    fc2_weight = normal_values(key_list[12], (FFN, C), FFN ** -0.5, 0.1875)
    return {"features": features, "neighbours": neighbours, "counts": counts, "block_dest": block_dest, "conv_weight": conv_weight, "cpe_weight": cpe_weight, "cpe_gain": cpe_gain, "norm1_gain": norm1_gain, "qkv_weight": qkv_weight, "proj_weight": proj_weight, "norm2_gain": norm2_gain, "fc1_weight": fc1_weight, "fc2_weight": fc2_weight}


def layer_norm(values, scale_gain):
    centre = values - lax.optimization_barrier(jnp.mean(values, axis=-1, keepdims=True))
    spread = lax.optimization_barrier(jnp.mean(centre * centre, axis=-1, keepdims=True))
    return centre * lax.rsqrt(spread + 1e-05) * scale_gain

def attend_patch(queries, key_rows, value_rows, key_live):
    length = queries.shape[0]
    query_heads = queries.reshape(length, HEADS, HEAD_DIM).astype(jnp.float32)
    key_heads = key_rows.reshape(length, HEADS, HEAD_DIM).astype(jnp.float32)
    value_heads = value_rows.reshape(length, HEADS, HEAD_DIM).astype(jnp.float32)

    def one_group(group_index):
        q_part = lax.dynamic_slice_in_dim(query_heads, group_index * 2, 2, 1)
        k_part = lax.dynamic_slice_in_dim(key_heads, group_index * 2, 2, 1)
        v_part = lax.dynamic_slice_in_dim(value_heads, group_index * 2, 2, 1)
        scores = jnp.einsum('qhd,khd->hqk', q_part, k_part) * HEAD_DIM ** (-0.5)
        scores = jnp.where(key_live[None, None, :], scores, jnp.float32(-1e+30))
        row_max = lax.optimization_barrier(jnp.max(scores, axis=-1, keepdims=True))
        exp_scores = jnp.exp(scores - row_max)
        weights = (exp_scores / lax.optimization_barrier(jnp.sum(exp_scores, axis=-1, keepdims=True))).astype(jnp.bfloat16)
        group_out = jnp.einsum('hqk,khd->qhd', weights.astype(jnp.float32), v_part)
        return group_out.astype(jnp.bfloat16)
    pieces = lax.map(one_group, jnp.arange(HEADS // 2, dtype=jnp.int32))
    return jnp.transpose(pieces, (1, 0, 2, 3)).reshape(length, HEADS * HEAD_DIM)

def reference(features, neighbours, counts, block_dest, conv_weight, cpe_weight, cpe_gain, norm1_gain, qkv_weight, proj_weight, norm2_gain, fc1_weight, fc2_weight):
    devices = GRID_X * GRID_Y
    local_rows = features.reshape(devices, ROWS, C)
    tap_rows = neighbours.reshape(devices, 27, ROWS)

    def position_encode(pair_in):
        rows_in, taps_in = pair_in
        padded = jnp.concatenate([rows_in, jnp.zeros((1, C), jnp.bfloat16)], axis=0)

        def add_tap(tap_index, running):
            picked = jnp.take(padded, taps_in[tap_index], axis=0)
            return running + jnp.dot(picked, conv_weight[tap_index], preferred_element_type=jnp.float32)
        summed = lax.fori_loop(0, 27, add_tap, jnp.zeros((ROWS, C), jnp.float32))
        conv_out = summed.astype(jnp.bfloat16)
        linear = jnp.dot(conv_out, cpe_weight, preferred_element_type=jnp.float32)
        return (rows_in.astype(jnp.float32) + layer_norm(linear, cpe_gain)).astype(jnp.bfloat16)
    encoded = lax.map(position_encode, (local_rows, tap_rows))
    block_span = BLOCK * C
    flat_dest = block_dest.reshape(-1).astype(jnp.int32)
    reordered = jnp.zeros((devices * NB, block_span), jnp.bfloat16).at[flat_dest].set(encoded.reshape(devices * NB, block_span))
    reordered = reordered.reshape(devices, ROWS, C)
    live_counts = counts.reshape(-1).astype(jnp.int32)
    offsets = (jnp.cumsum(live_counts) - live_counts).astype(jnp.int32)
    grand_total = jnp.sum(live_counts).astype(jnp.int32)
    row_index = jnp.arange(ROWS, dtype=jnp.int32)
    live_rows = row_index[None, :] < live_counts[:, None]
    patch_total = (devices * ROWS + PATCH - 1) // PATCH
    seq_length = patch_total * PATCH
    position = jnp.where(live_rows, offsets[:, None] + row_index[None, :], seq_length).astype(jnp.int32)
    sequence = jnp.zeros((seq_length, C), jnp.bfloat16).at[position.reshape(-1)].set(reordered.reshape(-1, C), mode='drop')

    def one_patch(patch_index):
        patch_rows = lax.dynamic_slice_in_dim(sequence, patch_index * PATCH, PATCH, 0)
        normed = layer_norm(patch_rows.astype(jnp.float32), norm1_gain).astype(jnp.bfloat16)
        projected = jnp.dot(normed, qkv_weight, preferred_element_type=jnp.float32).astype(jnp.bfloat16)
        key_live = patch_index * PATCH + jnp.arange(PATCH, dtype=jnp.int32) < grand_total
        return attend_patch(projected[:, :C], projected[:, C:2 * C], projected[:, 2 * C:], key_live)
    attended_seq = lax.map(one_patch, jnp.arange(patch_total, dtype=jnp.int32)).reshape(seq_length, C)
    gathered = jnp.take(attended_seq, jnp.minimum(position, seq_length - 1).reshape(-1), axis=0).reshape(devices, ROWS, C)
    attended = jnp.where(live_rows[:, :, None], gathered, jnp.zeros((), jnp.bfloat16))

    def finish(pair_in):
        rows_in, attn_rows = pair_in
        mixed_rows = (rows_in.astype(jnp.float32) + jnp.dot(attn_rows, proj_weight, preferred_element_type=jnp.float32)).astype(jnp.bfloat16)
        normed = layer_norm(mixed_rows.astype(jnp.float32), norm2_gain).astype(jnp.bfloat16)
        hidden = jax.nn.gelu(jnp.dot(normed, fc1_weight, preferred_element_type=jnp.float32), approximate=False).astype(jnp.bfloat16)
        return (mixed_rows.astype(jnp.float32) + jnp.dot(hidden, fc2_weight, preferred_element_type=jnp.float32)).astype(jnp.bfloat16)
    block_out = lax.map(finish, (reordered, attended))
    return block_out.reshape(GRID_X, GRID_Y, ROWS, C)
```

```python
import functools

import jax
import jax.numpy as jnp
from jax import lax
from jax.experimental import pallas as pl
from jax.experimental.pallas import tpu as pltpu
from jax.sharding import PartitionSpec as P

HEADS = 16
PATCH = 1024
BLOCK = 16
SUPER = 512
TILE = 128
WINDOW = 256
QTILE = 256
LANES = 128
AXES = ("gx", "gy")


def normalised(values, gain):
    centre = values - jnp.mean(values, axis=-1, keepdims=True)
    spread = jnp.mean(centre * centre, axis=-1, keepdims=True)
    return centre * lax.rsqrt(spread + 1e-05) * gain


def put(ref, start, value):
    for half in range(ref.shape[0]):
        ref[half, pl.ds(start, value.shape[0]), :] = value[:, half * LANES : (half + 1) * LANES]


def get(ref, start, size):
    return jnp.concatenate([ref[half, pl.ds(start, size), :] for half in range(ref.shape[0])], axis=1)


def conv_kernel(dest_ref, taps_ref, rows_ref, weight_ref, cpe_ref, gain_ref, out_ref, picked_ref):
    taps, span = taps_ref.shape
    total, width = rows_ref.shape
    step = pl.program_id(0)
    lanes = lax.broadcasted_iota(jnp.int32, (TILE, WINDOW), 1)

    for part in range(span // TILE):
        chunk = taps_ref[:, part * TILE : (part + 1) * TILE]
        as_float = chunk.astype(jnp.float32)
        low = jnp.min(as_float).astype(jnp.int32)
        high = jnp.max(jnp.where(chunk < total, as_float, -1.0)).astype(jnp.int32)
        low = low // BLOCK * BLOCK
        passes = (high - low + WINDOW) // WINDOW
        low = jnp.minimum(low, total - passes * WINDOW)
        filled = jnp.concatenate(
            [chunk, jnp.full((-taps % 8, TILE), total, jnp.int32)], axis=0
        )
        columns = filled.T
        here = pl.ds(part * TILE, TILE)

        def pick(start):
            window = rows_ref[pl.ds(pl.multiple_of(start, BLOCK), WINDOW), :]
            shifted = columns - start
            hot = jnp.concatenate(
                [
                    jnp.where(shifted[:, tap : tap + 1] == lanes, 1.0, 0.0).astype(jnp.bfloat16)
                    for tap in range(taps)
                ],
                axis=0,
            )
            return jnp.dot(hot, window, preferred_element_type=jnp.float32).astype(jnp.bfloat16)

        first = pick(low)
        for tap in range(taps):
            picked_ref[here, tap * width : (tap + 1) * width] = first[tap * TILE : (tap + 1) * TILE]

        @pl.loop(1, passes)
        def _(index):
            more = pick(low + index * WINDOW)
            for tap in range(taps):
                columns_here = slice(tap * width, (tap + 1) * width)
                picked_ref[here, columns_here] += more[tap * TILE : (tap + 1) * TILE]

    summed = jnp.dot(picked_ref[...], weight_ref[...], preferred_element_type=jnp.float32)
    linear = jnp.dot(
        summed.astype(jnp.bfloat16), cpe_ref[...], preferred_element_type=jnp.float32
    )
    own = rows_ref[pl.ds(pl.multiple_of(step * span, span), span), :].astype(jnp.float32)
    encoded = (own + normalised(linear, gain_ref[...])).astype(jnp.bfloat16)
    for block in range(span // BLOCK):
        place = dest_ref[step * (span // BLOCK) + block]
        out_ref[place] = encoded[block * BLOCK : (block + 1) * BLOCK]


def convolved(features, neighbours, dest, conv_weight, cpe_weight, cpe_gain):
    total, width = features.shape
    taps = neighbours.shape[0]
    blocks = total // BLOCK
    whole = lambda step, *_: (0, 0)
    return pl.pallas_call(
        conv_kernel,
        out_shape=jax.ShapeDtypeStruct((blocks, BLOCK, width), jnp.bfloat16),
        grid_spec=pltpu.PrefetchScalarGridSpec(
            num_scalar_prefetch=1,
            grid=(total // SUPER,),
            in_specs=[
                pl.BlockSpec((taps, SUPER), lambda step, *_: (0, step)),
                pl.BlockSpec((total, width), whole),
                pl.BlockSpec((taps * width, width), whole),
                pl.BlockSpec((width, width), whole),
                pl.BlockSpec((1, width), whole),
            ],
            out_specs=pl.BlockSpec((blocks, BLOCK, width), lambda step, *_: (0, 0, 0)),
            scratch_shapes=[pltpu.VMEM((SUPER, taps * width), jnp.bfloat16)],
        ),
        compiler_params=pltpu.CompilerParams(vmem_limit_bytes=56 << 20),
        name="convolve",
    )(dest, neighbours, features, conv_weight, cpe_weight, cpe_gain)


def place_kernel(slots_ref, count_ref, arrived_ref, moved_ref, tail_ref, wide_ref):
    blocks = arrived_ref.shape[0]

    @pl.loop(0, blocks)
    def _(source):
        row = pl.multiple_of(slots_ref[source] * BLOCK, BLOCK)
        block = arrived_ref[source]
        moved_ref[pl.ds(row, BLOCK), :] = block
        put(wide_ref, row, block.astype(jnp.float32))

    start = count_ref[0] - PATCH
    for part in range(PATCH // QTILE):
        tail_ref[part * QTILE : (part + 1) * QTILE, :] = get(
            wide_ref, start + part * QTILE, QTILE
        ).astype(jnp.bfloat16)


def placed_rows(slots, count, arrived):
    blocks, block, width = arrived.shape
    vmem = pl.BlockSpec(memory_space=pltpu.VMEM)
    smem = pl.BlockSpec(memory_space=pltpu.SMEM)
    return pl.pallas_call(
        place_kernel,
        out_shape=(
            jax.ShapeDtypeStruct((blocks * block, width), jnp.bfloat16),
            jax.ShapeDtypeStruct((PATCH, width), jnp.bfloat16),
        ),
        in_specs=[smem, smem, vmem],
        out_specs=(vmem, vmem),
        scratch_shapes=[pltpu.VMEM((width // LANES, blocks * block, LANES), jnp.float32)],
        compiler_params=pltpu.CompilerParams(vmem_limit_bytes=32 << 20),
        name="place",
    )(slots, count, arrived)


def block_kernel(
    scalars_ref,
    moved_ref,
    tail_ref,
    head_ref,
    gain_one_ref,
    qkv_ref,
    proj_ref,
    gain_two_ref,
    fc_one_ref,
    fc_two_ref,
    out_ref,
    source_ref,
    own_ref,
    keys_ref,
    values_ref,
    result_ref,
    gathered_ref,
):
    rows, width = moved_ref.shape
    skew = scalars_ref[0]
    live = scalars_ref[1]
    known = scalars_ref[2]
    live_end = skew + live

    for part in range(PATCH // QTILE):
        piece = tail_ref[part * QTILE : (part + 1) * QTILE, :].astype(jnp.float32)
        put(source_ref, skew + part * QTILE, piece)
    for part in range(rows // QTILE):
        piece = moved_ref[part * QTILE : (part + 1) * QTILE, :].astype(jnp.float32)
        put(source_ref, PATCH + skew + part * QTILE, piece)
        put(own_ref, skew + part * QTILE, piece)
    for part in range(PATCH // QTILE):
        piece = head_ref[part * QTILE : (part + 1) * QTILE, :].astype(jnp.float32)
        put(source_ref, PATCH + live_end + part * QTILE, piece)

    per_patch = PATCH // QTILE
    patches = (live_end + PATCH - 1) // PATCH

    @pl.loop(0, patches)
    def _(patch):
        for part in range(per_patch):
            start = pl.multiple_of(PATCH + patch * PATCH + part * QTILE, QTILE)
            normed = normalised(get(source_ref, start, QTILE), gain_one_ref[...])
            pair = jnp.dot(
                normed.astype(jnp.bfloat16),
                qkv_ref[:, width:],
                preferred_element_type=jnp.float32,
            )
            columns = slice(part * QTILE, (part + 1) * QTILE)
            keys_ref[patch, :, columns] = pair[:, :width].T.astype(jnp.bfloat16)
            values_ref[patch, columns, :] = pair[:, width:].astype(jnp.bfloat16)

    head_of_lane = lax.broadcasted_iota(jnp.int32, (QTILE, width), 1) // (width // HEADS)

    @pl.loop(skew // QTILE, (skew + rows + QTILE - 1) // QTILE)
    def _(tile):
        start = pl.multiple_of(tile * QTILE, QTILE)
        here = get(own_ref, start, QTILE)
        gathered_ref[...] = jnp.zeros((QTILE, width), jnp.float32)

        @pl.when(start < live_end)
        def _():
            patch = tile // per_patch
            normed = normalised(here, gain_one_ref[...]).astype(jnp.bfloat16)
            queries = jnp.dot(normed, qkv_ref[:, :width], preferred_element_type=jnp.float32)
            queries = queries.astype(jnp.bfloat16) * jnp.bfloat16((width // HEADS) ** -0.5)
            spot = patch * PATCH + lax.broadcasted_iota(jnp.int32, (1, PATCH), 1)
            bias = jnp.where(spot < known, 0.0, -1e30)

            @pl.loop(0, HEADS)
            def _(head):
                mine = head_of_lane == head
                one = jnp.where(mine, queries, jnp.bfloat16(0))
                scores = jnp.dot(one, keys_ref[patch], preferred_element_type=jnp.float32) + bias
                top = jnp.max(scores, axis=-1, keepdims=True)
                grown = jnp.exp(scores - top)
                share = jnp.sum(grown, axis=-1, keepdims=True)
                mixed = jnp.dot(
                    grown.astype(jnp.bfloat16), values_ref[patch], preferred_element_type=jnp.float32
                )
                gathered_ref[...] = jnp.where(mine, mixed / share, gathered_ref[...])

        spots = start + lax.broadcasted_iota(jnp.int32, (QTILE, 1), 0)
        attended = jnp.where(spots < live_end, gathered_ref[...], 0.0)
        projected = jnp.dot(
            attended.astype(jnp.bfloat16), proj_ref[...], preferred_element_type=jnp.float32
        )
        mixed = (here + projected).astype(jnp.bfloat16).astype(jnp.float32)
        normed = normalised(mixed, gain_two_ref[...]).astype(jnp.bfloat16)
        hidden = jnp.dot(normed, fc_one_ref[...], preferred_element_type=jnp.float32)
        hidden = 0.5 * hidden * (1.0 + lax.erf(hidden * 0.5**0.5))
        final = mixed + jnp.dot(
            hidden.astype(jnp.bfloat16), fc_two_ref[...], preferred_element_type=jnp.float32
        )
        put(result_ref, start, final)

    for part in range(rows // QTILE):
        out_ref[part * QTILE : (part + 1) * QTILE, :] = get(
            result_ref, skew + part * QTILE, QTILE
        ).astype(jnp.bfloat16)


def finished(scalars, moved, tail, head, gain_one, qkv, proj, gain_two, fc_one, fc_two):
    rows, width = moved.shape
    vmem = pl.BlockSpec(memory_space=pltpu.VMEM)
    smem = pl.BlockSpec(memory_space=pltpu.SMEM)
    most = rows // PATCH + 1
    halves = width // LANES
    return pl.pallas_call(
        block_kernel,
        out_shape=jax.ShapeDtypeStruct((rows, width), jnp.bfloat16),
        in_specs=[smem] + [vmem] * 9,
        out_specs=vmem,
        scratch_shapes=[
            pltpu.VMEM((halves, (most + 2) * PATCH, LANES), jnp.float32),
            pltpu.VMEM((halves, most * PATCH, LANES), jnp.float32),
            pltpu.VMEM((most, width, PATCH), jnp.bfloat16),
            pltpu.VMEM((most, PATCH, width), jnp.bfloat16),
            pltpu.VMEM((halves, most * PATCH, LANES), jnp.float32),
            pltpu.VMEM((QTILE, width), jnp.float32),
        ],
        compiler_params=pltpu.CompilerParams(vmem_limit_bytes=56 << 20),
        name="attend",
    )(scalars, moved, tail, head, gain_one, qkv, proj, gain_two, fc_one, fc_two)


def passed_along(shard, by):
    count = lax.axis_size(AXES)
    pairs = [(i, i + by) for i in range(count) if 0 <= i + by < count]
    return lax.ppermute(shard, AXES, pairs)


def per_device(
    features,
    neighbours,
    counts,
    block_dest,
    conv_weight,
    cpe_weight,
    cpe_gain,
    norm1_gain,
    qkv_weight,
    proj_weight,
    norm2_gain,
    fc1_weight,
    fc2_weight,
):
    rows, width = features.shape[2:]
    taps = neighbours.shape[2]
    blocks = block_dest.shape[2]
    devices = lax.axis_size(AXES)
    me = lax.axis_index(AXES)
    own_count = counts.reshape(1)
    place = block_dest.reshape(blocks)
    target = place // blocks
    label = jnp.stack([place % blocks, jnp.broadcast_to(own_count, (blocks,))], axis=1)
    labels = jnp.zeros((devices, 2), jnp.int32).at[target].set(label)
    labels = lax.all_to_all(labels, AXES, split_axis=0, concat_axis=0, tiled=True)
    slots, every_count = labels[:, 0], labels[:, 1]
    outgoing = convolved(
        features.reshape(rows, width),
        neighbours.reshape(taps, rows),
        target,
        conv_weight.reshape(taps * width, width),
        cpe_weight,
        cpe_gain.reshape(1, width),
    )
    arrived = lax.all_to_all(outgoing, AXES, split_axis=0, concat_axis=0, tiled=True)
    moved, tail = placed_rows(slots, own_count, arrived)
    before = passed_along(tail, 1)
    after = passed_along(moved[:PATCH], -1)
    earlier = jnp.arange(devices) < me
    offset = jnp.sum(jnp.where(earlier, every_count, 0))
    known = jnp.sum(jnp.where(earlier, 0, every_count))
    skew = offset % PATCH
    scalars = jnp.stack([skew, own_count[0], known + skew])
    block_out = finished(
        scalars,
        moved,
        before,
        after,
        norm1_gain.reshape(1, width),
        qkv_weight,
        proj_weight,
        norm2_gain.reshape(1, width),
        fc1_weight,
        fc2_weight,
    )
    return block_out.reshape(1, 1, rows, width)


def solution(mesh):
    placed = (
        P("gx", "gy", None, None),
        P("gx", "gy", None, None),
        P("gx", "gy"),
        P("gx", "gy", None),
    ) + (P(),) * 9
    return jax.shard_map(
        per_device, mesh=mesh, in_specs=placed, out_specs=P("gx", "gy", None, None), check_vma=False
    )
```

```python
import jax
import jax.numpy as jnp
from jax import lax
from jax.experimental import pallas as pl
from jax.experimental.pallas import tpu as pltpu
from jax.sharding import PartitionSpec as P

HEADS = 16
PATCH = 1024
BLOCK = 16
SUPER = 512
TILE = 128
WINDOW = 256
QTILE = 256
LANES = 128
SAFE_SCORE = 30.0
SAFE_VALUE = 1e20


def normalised(values, gain):
    centre = values - jnp.mean(values, axis=-1, keepdims=True)
    spread = jnp.mean(centre * centre, axis=-1, keepdims=True)
    return centre * lax.rsqrt(spread + 1e-05) * gain


def put(ref, start, value):
    for half in range(ref.shape[0]):
        ref[half, pl.ds(start, value.shape[0]), :] = value[:, half * LANES : (half + 1) * LANES]


def get(ref, start, size):
    return jnp.concatenate([ref[half, pl.ds(start, size), :] for half in range(ref.shape[0])], axis=1)


def conv_kernel(
    dest_ref,
    count_ref,
    taps_ref,
    rows_ref,
    weight_ref,
    cpe_ref,
    gain_ref,
    out_ref,
    notes_ref,
    picked_ref,
):
    taps, span = taps_ref.shape
    total, width = rows_ref.shape
    blocks = out_ref.shape[0]
    step = pl.program_id(0)
    note_lane = lax.broadcasted_iota(jnp.int32, (1, LANES), 1)
    lanes = lax.broadcasted_iota(jnp.int32, (TILE, WINDOW), 1)

    for part in range(span // TILE):
        chunk = taps_ref[:, part * TILE : (part + 1) * TILE]
        as_float = chunk.astype(jnp.float32)
        low = jnp.min(as_float).astype(jnp.int32)
        high = jnp.max(jnp.where(chunk < total, as_float, -1.0)).astype(jnp.int32)
        low = low // BLOCK * BLOCK
        passes = (high - low + WINDOW) // WINDOW
        low = jnp.minimum(low, total - passes * WINDOW)
        filled = jnp.concatenate(
            [chunk, jnp.full((-taps % 8, TILE), total, jnp.int32)], axis=0
        )
        columns = filled.T
        here = pl.ds(part * TILE, TILE)

        def pick(start):
            window = rows_ref[pl.ds(pl.multiple_of(start, BLOCK), WINDOW), :]
            shifted = columns - start
            hot = jnp.concatenate(
                [
                    jnp.where(shifted[:, tap : tap + 1] == lanes, 1.0, 0.0).astype(jnp.bfloat16)
                    for tap in range(taps)
                ],
                axis=0,
            )
            return jnp.dot(hot, window, preferred_element_type=jnp.float32).astype(jnp.bfloat16)

        first = pick(low)
        for tap in range(taps):
            picked_ref[here, tap * width : (tap + 1) * width] = first[tap * TILE : (tap + 1) * TILE]

        @pl.loop(1, passes)
        def _(index):
            more = pick(low + index * WINDOW)
            for tap in range(taps):
                columns_here = slice(tap * width, (tap + 1) * width)
                picked_ref[here, columns_here] += more[tap * TILE : (tap + 1) * TILE]

    summed = jnp.dot(picked_ref[...], weight_ref[...], preferred_element_type=jnp.float32)
    linear = jnp.dot(
        summed.astype(jnp.bfloat16), cpe_ref[...], preferred_element_type=jnp.float32
    )
    own = rows_ref[pl.ds(pl.multiple_of(step * span, span), span), :].astype(jnp.float32)
    encoded = (own + normalised(linear, gain_ref[...])).astype(jnp.bfloat16)
    for block in range(span // BLOCK):
        place = dest_ref[step * (span // BLOCK) + block]
        target, slot = place // blocks, place % blocks
        out_ref[target] = encoded[block * BLOCK : (block + 1) * BLOCK]
        notes_ref[target] = jnp.where(note_lane == 0, slot, count_ref[0])


def convolved(features, neighbours, dest, count, conv_weight, cpe_weight, cpe_gain):
    total, width = features.shape
    taps = neighbours.shape[0]
    blocks = total // BLOCK
    whole = lambda step, *_: (0, 0)
    return pl.pallas_call(
        conv_kernel,
        out_shape=(
            jax.ShapeDtypeStruct((blocks, BLOCK, width), jnp.bfloat16),
            jax.ShapeDtypeStruct((blocks, 1, LANES), jnp.int32),
        ),
        grid_spec=pltpu.PrefetchScalarGridSpec(
            num_scalar_prefetch=2,
            grid=(total // SUPER,),
            in_specs=[
                pl.BlockSpec((taps, SUPER), lambda step, *_: (0, step)),
                pl.BlockSpec((total, width), whole),
                pl.BlockSpec((taps * width, width), whole),
                pl.BlockSpec((width, width), whole),
                pl.BlockSpec((1, width), whole),
            ],
            out_specs=(
                pl.BlockSpec((blocks, BLOCK, width), lambda step, *_: (0, 0, 0)),
                pl.BlockSpec((blocks, 1, LANES), lambda step, *_: (0, 0, 0)),
            ),
            scratch_shapes=[pltpu.VMEM((SUPER, taps * width), jnp.bfloat16)],
        ),
        compiler_params=pltpu.CompilerParams(vmem_limit_bytes=56 << 20),
        name="convolve",
    )(dest, count, neighbours, features, conv_weight, cpe_weight, cpe_gain)


def exchange_kernel(
    count_ref,
    outgoing_ref,
    notes_ref,
    moved_ref,
    before_ref,
    after_ref,
    summary_ref,
    arrived_ref,
    heard_ref,
    wide_ref,
    tail_ref,
    index_ref,
    order_ref,
    send_sem,
    recv_sem,
    note_send_sem,
    note_recv_sem,
    side_send_sem,
    side_recv_sem,
    local_sem,
):
    devices = outgoing_ref.shape[0]
    across = lax.axis_size("gy")
    me = lax.axis_index("gx") * across + lax.axis_index("gy")

    def place_of(device):
        return (device // across, device % across)

    def to_peer(source, sink, sems, device):
        return pltpu.make_async_remote_copy(
            src_ref=source,
            dst_ref=sink,
            send_sem=sems[0],
            recv_sem=sems[1],
            device_id=place_of(device),
            device_id_type=pl.DeviceIdType.MESH,
        )

    block_sems = (send_sem, recv_sem)
    note_sems = (note_send_sem, note_recv_sem)

    def send(step, _):
        peer = (me + step) % devices
        to_peer(notes_ref.at[peer], heard_ref.at[me], note_sems, peer).start()
        to_peer(outgoing_ref.at[peer], arrived_ref.at[me], block_sems, peer).start()
        return 0

    lax.fori_loop(1, devices, send, 0)
    arrived_ref[me] = outgoing_ref[me]
    heard_ref[me] = notes_ref[me]
    others = pl.ds(0, devices - 1)
    all_notes = to_peer(notes_ref.at[others], heard_ref.at[others], note_sems, me)
    all_notes.wait_recv()

    heard = heard_ref[...].reshape(devices, LANES)
    source = lax.broadcasted_iota(jnp.int32, (devices, LANES), 0)
    lane = lax.broadcasted_iota(jnp.int32, (devices, LANES), 1)
    slots = heard[:, :1]
    index_ref[...] = jnp.max(jnp.where(slots == lane, source, 0), axis=0, keepdims=True)
    counts = heard[:, 1:2]
    offset = jnp.sum(jnp.where(source < me, counts, 0), axis=0, keepdims=True)
    rest = jnp.sum(jnp.where(source < me, 0, counts), axis=0, keepdims=True)
    summary_ref[...] = jnp.where(lane[:1] == 0, offset, rest)
    order = pltpu.make_async_copy(index_ref, order_ref, local_sem)
    order.start()
    order.wait()

    all_blocks = to_peer(outgoing_ref.at[others], arrived_ref.at[others], block_sems, me)
    all_blocks.wait_recv()

    def settle(slot, _):
        block = arrived_ref[order_ref[0, slot]]
        row = pl.multiple_of(slot * BLOCK, BLOCK)
        moved_ref[pl.ds(row, BLOCK), :] = block
        put(wide_ref, row, block.astype(jnp.float32))
        return 0

    lax.fori_loop(0, devices, settle, 0)
    following = (me + 1) % devices
    previous = (me + devices - 1) % devices
    head_sems = (side_send_sem.at[0], side_recv_sem.at[0])
    tail_sems = (side_send_sem.at[1], side_recv_sem.at[1])
    head = to_peer(moved_ref.at[pl.ds(0, PATCH)], after_ref, head_sems, previous)
    head.start()
    start = jnp.clip(count_ref[0] - PATCH, 0, moved_ref.shape[0] - PATCH)
    for part in range(PATCH // QTILE):
        piece = get(wide_ref, start + part * QTILE, QTILE)
        tail_ref[part * QTILE : (part + 1) * QTILE, :] = piece.astype(jnp.bfloat16)
    tail = to_peer(tail_ref, before_ref, tail_sems, following)
    tail.start()
    all_notes.wait_send()
    all_blocks.wait_send()
    head.wait()
    tail.wait()


def exchanged(count, outgoing, notes):
    blocks, block, width = outgoing.shape
    rows = blocks * block
    vmem = pl.BlockSpec(memory_space=pltpu.VMEM)
    smem = pl.BlockSpec(memory_space=pltpu.SMEM)
    side = jax.ShapeDtypeStruct((PATCH, width), jnp.bfloat16)
    dma = pltpu.SemaphoreType.DMA
    return pl.pallas_call(
        exchange_kernel,
        out_shape=(
            jax.ShapeDtypeStruct((rows, width), jnp.bfloat16),
            side,
            side,
            jax.ShapeDtypeStruct((1, LANES), jnp.int32),
        ),
        in_specs=[smem, vmem, vmem],
        out_specs=(vmem, vmem, vmem, vmem),
        scratch_shapes=[
            pltpu.VMEM((blocks, block, width), jnp.bfloat16),
            pltpu.VMEM((blocks, 1, LANES), jnp.int32),
            pltpu.VMEM((width // LANES, rows, LANES), jnp.float32),
            pltpu.VMEM((PATCH, width), jnp.bfloat16),
            pltpu.VMEM((1, LANES), jnp.int32),
            pltpu.SMEM((1, LANES), jnp.int32),
            dma,
            dma,
            dma,
            dma,
            dma((2,)),
            dma((2,)),
            dma,
        ],
        compiler_params=pltpu.CompilerParams(
            vmem_limit_bytes=32 << 20, has_side_effects=True
        ),
        name="exchange",
    )(count, outgoing, notes)


def block_kernel(
    summary_ref,
    count_ref,
    moved_ref,
    tail_ref,
    head_ref,
    gain_one_ref,
    qkv_ref,
    proj_ref,
    gain_two_ref,
    fc_one_ref,
    fc_two_ref,
    out_ref,
    source_ref,
    own_ref,
    keys_ref,
    values_ref,
    result_ref,
    gathered_ref,
    reach_ref,
    size_ref,
):
    rows, width = moved_ref.shape
    skew = summary_ref[0, 0] % PATCH
    live = count_ref[0]
    known = summary_ref[0, 1] + skew
    live_end = skew + live

    for part in range(PATCH // QTILE):
        piece = tail_ref[part * QTILE : (part + 1) * QTILE, :].astype(jnp.float32)
        put(source_ref, skew + part * QTILE, piece)
    for part in range(rows // QTILE):
        piece = moved_ref[part * QTILE : (part + 1) * QTILE, :].astype(jnp.float32)
        put(source_ref, PATCH + skew + part * QTILE, piece)
        put(own_ref, skew + part * QTILE, piece)
    for part in range(PATCH // QTILE):
        piece = head_ref[part * QTILE : (part + 1) * QTILE, :].astype(jnp.float32)
        put(source_ref, PATCH + live_end + part * QTILE, piece)

    head_of_lane = lax.broadcasted_iota(jnp.int32, (QTILE, width), 1) // (width // HEADS)
    left = lax.broadcasted_iota(jnp.int32, (width, width), 0) // (width // HEADS)
    right = lax.broadcasted_iota(jnp.int32, (width, width), 1) // (width // HEADS)
    same_head = jnp.where(left == right, 1.0, 0.0).astype(jnp.bfloat16)

    def squares(values):
        values = values.astype(jnp.float32)
        total = jnp.dot(
            (values * values).astype(jnp.bfloat16), same_head, preferred_element_type=jnp.float32
        )
        return 1.02 * total

    per_patch = PATCH // QTILE
    patches = (live_end + PATCH - 1) // PATCH

    @pl.loop(0, patches)
    def _(patch):
        for part in range(per_patch):
            start = pl.multiple_of(PATCH + patch * PATCH + part * QTILE, QTILE)
            normed = normalised(get(source_ref, start, QTILE), gain_one_ref[...])
            pair = jnp.dot(
                normed.astype(jnp.bfloat16),
                qkv_ref[:, width:],
                preferred_element_type=jnp.float32,
            )
            columns = slice(part * QTILE, (part + 1) * QTILE)
            some_keys = pair[:, :width].astype(jnp.bfloat16).astype(jnp.float32)
            keys_ref[patch, :, columns] = some_keys.T.astype(jnp.bfloat16)
            alive = start - PATCH + lax.broadcasted_iota(jnp.int32, (QTILE, 1), 0) < known
            some_values = pair[:, width:].astype(jnp.bfloat16)
            for odd in range(2):
                fitted = jnp.where(head_of_lane % 2 == odd, some_values, jnp.bfloat16(1))
                values_ref[patch, odd, columns, :] = jnp.where(alive, fitted, jnp.bfloat16(0))
            reach = jnp.max(squares(some_keys), axis=0, keepdims=True)
            size = jnp.max(jnp.abs(pair[:, width:]), axis=0, keepdims=True)
            reach_ref[patch] = reach if part == 0 else jnp.maximum(reach_ref[patch], reach)
            size_ref[patch] = size if part == 0 else jnp.maximum(size_ref[patch], size)


    @pl.loop(skew // QTILE, (skew + rows + QTILE - 1) // QTILE)
    def _(tile):
        start = pl.multiple_of(tile * QTILE, QTILE)
        here = get(own_ref, start, QTILE)
        gathered_ref[...] = jnp.zeros((QTILE, width), jnp.float32)

        @pl.when(start < live_end)
        def _():
            patch = tile // per_patch
            normed = normalised(here, gain_one_ref[...]).astype(jnp.bfloat16)
            queries = jnp.dot(normed, qkv_ref[:, :width], preferred_element_type=jnp.float32)
            queries = queries.astype(jnp.bfloat16) * jnp.bfloat16((width // HEADS) ** -0.5)
            reach = jnp.max(squares(queries) * reach_ref[patch])
            safe = (reach <= SAFE_SCORE**2) & (jnp.max(size_ref[patch]) <= SAFE_VALUE)

            def gather(group, odd, softened):
                heads = [2 * (group * 2 + index) + odd for index in range(2)]
                one = jnp.concatenate(
                    [jnp.where(head_of_lane == head, queries, jnp.bfloat16(0)) for head in heads],
                    axis=0,
                )
                scores = jnp.dot(one, keys_ref[patch], preferred_element_type=jnp.float32)
                grown = softened(scores).astype(jnp.bfloat16)
                mixed = jnp.dot(grown, values_ref[patch, odd], preferred_element_type=jnp.float32)
                spare = LANES - 1 if odd == 0 else 0
                mixed = mixed * (1.0 / mixed[:, spare : spare + 1])
                so_far = gathered_ref[...]
                for index, head in enumerate(heads):
                    piece = mixed[index * QTILE : (index + 1) * QTILE]
                    so_far = jnp.where(head_of_lane == head, piece, so_far)
                gathered_ref[...] = so_far

            @pl.when(safe)
            def _():
                @pl.loop(0, HEADS // 4, unroll=4)
                def _(group):
                    for odd in range(2):
                        gather(group, odd, jnp.exp)

            @pl.when(jnp.logical_not(safe))
            def _():
                spot = patch * PATCH + lax.broadcasted_iota(jnp.int32, (1, PATCH), 1)
                bias = jnp.where(spot < known, 0.0, -1e30)

                def softened(scores):
                    scores = scores + bias
                    return jnp.exp(scores - jnp.max(scores, axis=-1, keepdims=True))

                @pl.loop(0, HEADS // 4)
                def _(group):
                    for odd in range(2):
                        gather(group, odd, softened)

        spots = start + lax.broadcasted_iota(jnp.int32, (QTILE, 1), 0)
        attended = jnp.where(spots < live_end, gathered_ref[...], 0.0)
        projected = jnp.dot(
            attended.astype(jnp.bfloat16), proj_ref[...], preferred_element_type=jnp.float32
        )
        mixed = (here + projected).astype(jnp.bfloat16).astype(jnp.float32)
        normed = normalised(mixed, gain_two_ref[...]).astype(jnp.bfloat16)
        hidden = jnp.dot(normed, fc_one_ref[...], preferred_element_type=jnp.float32)
        hidden = 0.5 * hidden * (1.0 + lax.erf(hidden * 0.5**0.5))
        final = mixed + jnp.dot(
            hidden.astype(jnp.bfloat16), fc_two_ref[...], preferred_element_type=jnp.float32
        )
        put(result_ref, start, final)

    for part in range(rows // QTILE):
        out_ref[part * QTILE : (part + 1) * QTILE, :] = get(
            result_ref, skew + part * QTILE, QTILE
        ).astype(jnp.bfloat16)


def finished(summary, count, moved, tail, head, gain_one, qkv, proj, gain_two, fc_one, fc_two):
    rows, width = moved.shape
    vmem = pl.BlockSpec(memory_space=pltpu.VMEM)
    smem = pl.BlockSpec(memory_space=pltpu.SMEM)
    most = rows // PATCH + 1
    halves = width // LANES
    return pl.pallas_call(
        block_kernel,
        out_shape=jax.ShapeDtypeStruct((rows, width), jnp.bfloat16),
        in_specs=[smem, smem] + [vmem] * 9,
        out_specs=vmem,
        scratch_shapes=[
            pltpu.VMEM((halves, (most + 2) * PATCH, LANES), jnp.float32),
            pltpu.VMEM((halves, most * PATCH, LANES), jnp.float32),
            pltpu.VMEM((most, width, PATCH), jnp.bfloat16),
            pltpu.VMEM((most, 2, PATCH, width), jnp.bfloat16),
            pltpu.VMEM((halves, most * PATCH, LANES), jnp.float32),
            pltpu.VMEM((QTILE, width), jnp.float32),
            pltpu.VMEM((most, 1, width), jnp.float32),
            pltpu.VMEM((most, 1, width), jnp.float32),
        ],
        compiler_params=pltpu.CompilerParams(vmem_limit_bytes=56 << 20),
        name="attend",
    )(summary, count, moved, tail, head, gain_one, qkv, proj, gain_two, fc_one, fc_two)


def per_device(
    features,
    neighbours,
    counts,
    block_dest,
    conv_weight,
    cpe_weight,
    cpe_gain,
    norm1_gain,
    qkv_weight,
    proj_weight,
    norm2_gain,
    fc1_weight,
    fc2_weight,
):
    rows, width = features.shape[2:]
    taps = neighbours.shape[2]
    own_count = counts.reshape(1)
    outgoing, notes = convolved(
        features.reshape(rows, width),
        neighbours.reshape(taps, rows),
        block_dest.reshape(-1),
        own_count,
        conv_weight.reshape(taps * width, width),
        cpe_weight,
        cpe_gain.reshape(1, width),
    )
    moved, before, after, summary = exchanged(own_count, outgoing, notes)
    block_out = finished(
        summary,
        own_count,
        moved,
        before,
        after,
        norm1_gain.reshape(1, width),
        qkv_weight,
        proj_weight,
        norm2_gain.reshape(1, width),
        fc1_weight,
        fc2_weight,
    )
    return block_out.reshape(1, 1, rows, width)


def solution(mesh):
    placed = (
        P("gx", "gy", None, None),
        P("gx", "gy", None, None),
        P("gx", "gy"),
        P("gx", "gy", None),
    ) + (P(),) * 9
    return jax.shard_map(
        per_device, mesh=mesh, in_specs=placed, out_specs=P("gx", "gy", None, None), check_vma=False
    )
```

```python
import functools

import jax
import jax.numpy as jnp
from jax import lax
from jax.experimental import pallas as pl
from jax.experimental.pallas import tpu as pltpu
from jax.sharding import PartitionSpec as P

HEADS = 16
PATCH = 1024
BLOCK = 16
SUPER = 1024
TILE = 128
WINDOW = 256
QTILE = 256
LANES = 128
STACK = 2
SAFE_SCORE = 30.0
SAFE_VALUE = 1e20


def normalised(values, gain):
    centre = values - jnp.mean(values, axis=-1, keepdims=True)
    spread = jnp.mean(centre * centre, axis=-1, keepdims=True)
    return centre * lax.rsqrt(spread + 1e-05) * gain


def put(ref, start, value):
    for half in range(ref.shape[0]):
        ref[half, pl.ds(start, value.shape[0]), :] = value[:, half * LANES : (half + 1) * LANES]


def get(ref, start, size):
    return jnp.concatenate([ref[half, pl.ds(start, size), :] for half in range(ref.shape[0])], axis=1)


def conv_kernel(
    dest_ref,
    count_ref,
    taps_ref,
    rows_ref,
    weight_ref,
    cpe_ref,
    gain_ref,
    out_ref,
    notes_ref,
    picked_ref,
    columns_ref,
    lows_ref,
    passes_ref,
    held_ref,
    held_sem,
):
    taps, span = taps_ref.shape
    total, width = rows_ref.shape
    blocks = out_ref.shape[0]
    step = pl.program_id(0)
    fetch = pltpu.make_async_copy(weight_ref, held_ref, held_sem)

    @pl.when(step == 0)
    def _():
        fetch.start()

    note_lane = lax.broadcasted_iota(jnp.int32, (1, LANES), 1)
    lanes = lax.broadcasted_iota(jnp.int32, (TILE, WINDOW), 1)

    def columns_of(part):
        chunk = taps_ref[:, part * TILE : (part + 1) * TILE]
        spare = jnp.full((-taps % 8, TILE), total, jnp.int32)
        return chunk, jnp.concatenate([chunk, spare], axis=0).T

    def reach(chunk):
        as_float = chunk.astype(jnp.float32)
        low = jnp.min(as_float).astype(jnp.int32) // BLOCK * BLOCK
        high = jnp.max(jnp.where(chunk < total, as_float, -1.0)).astype(jnp.int32)
        passes = (high - low + WINDOW) // WINDOW
        return jnp.minimum(low, total - passes * WINDOW), passes

    def pick(columns, start):
        window = rows_ref[pl.ds(pl.multiple_of(start, BLOCK), WINDOW), :]
        shifted = columns - start
        return [
            jnp.dot(
                jnp.where(shifted[:, tap : tap + 1] == lanes, 1.0, 0.0).astype(jnp.bfloat16),
                window,
                preferred_element_type=jnp.float32,
            ).astype(jnp.bfloat16)
            for tap in range(taps)
        ]

    parts = [columns_of(part) for part in range(span // TILE)]
    ranges = [reach(chunk) for chunk, _ in parts]
    for part, (low, passes) in enumerate(ranges):
        first = pick(parts[part][1], low)
        for tap in range(taps):
            picked_ref[part * TILE : (part + 1) * TILE, tap * width : (tap + 1) * width] = first[tap]
        lows_ref[part] = low
        passes_ref[part] = passes

    @pl.when(functools.reduce(jnp.maximum, [passes for _, passes in ranges]) > 1)
    def _():
        for part in range(span // TILE):
            columns_ref[part] = parts[part][1]

        @pl.loop(0, span // TILE)
        def _(part):
            here = pl.ds(pl.multiple_of(part * TILE, TILE), TILE)

            @pl.loop(1, passes_ref[part])
            def _(index):
                more = pick(columns_ref[part], lows_ref[part] + index * WINDOW)
                for tap in range(taps):
                    columns = slice(tap * width, (tap + 1) * width)
                    picked_ref[here, columns] += more[tap]

    @pl.when(step == 0)
    def _():
        fetch.wait()

    summed = jnp.dot(picked_ref[...], held_ref[...], preferred_element_type=jnp.float32)
    linear = jnp.dot(
        summed.astype(jnp.bfloat16), cpe_ref[...], preferred_element_type=jnp.float32
    )
    own = rows_ref[pl.ds(pl.multiple_of(step * span, span), span), :].astype(jnp.float32)
    encoded = (own + normalised(linear, gain_ref[...])).astype(jnp.bfloat16)
    for block in range(span // BLOCK):
        place = dest_ref[step * (span // BLOCK) + block]
        target, slot = place // blocks, place % blocks
        out_ref[target] = encoded[block * BLOCK : (block + 1) * BLOCK]
        notes_ref[target] = jnp.where(note_lane == 0, slot, count_ref[0])


def convolved(features, neighbours, dest, count, conv_weight, cpe_weight, cpe_gain):
    total, width = features.shape
    taps = neighbours.shape[0]
    blocks = total // BLOCK
    whole = lambda step, *_: (0, 0)
    return pl.pallas_call(
        conv_kernel,
        out_shape=(
            jax.ShapeDtypeStruct((blocks, BLOCK, width), jnp.bfloat16),
            jax.ShapeDtypeStruct((blocks, 1, LANES), jnp.int32),
        ),
        grid_spec=pltpu.PrefetchScalarGridSpec(
            num_scalar_prefetch=2,
            grid=(total // SUPER,),
            in_specs=[
                pl.BlockSpec((taps, SUPER), lambda step, *_: (0, step)),
                pl.BlockSpec((total, width), whole),
                pl.BlockSpec(memory_space=pltpu.HBM),
                pl.BlockSpec((width, width), whole),
                pl.BlockSpec((1, width), whole),
            ],
            out_specs=(
                pl.BlockSpec((blocks, BLOCK, width), lambda step, *_: (0, 0, 0)),
                pl.BlockSpec((blocks, 1, LANES), lambda step, *_: (0, 0, 0)),
            ),
            scratch_shapes=[
                pltpu.VMEM((SUPER, taps * width), jnp.bfloat16),
                pltpu.VMEM((SUPER // TILE, TILE, taps + -taps % 8), jnp.int32),
                pltpu.SMEM((SUPER // TILE,), jnp.int32),
                pltpu.SMEM((SUPER // TILE,), jnp.int32),
                pltpu.VMEM((taps * width, width), jnp.bfloat16),
                pltpu.SemaphoreType.DMA,
            ],
        ),
        compiler_params=pltpu.CompilerParams(vmem_limit_bytes=40 << 20),
        name="convolve",
    )(dest, count, neighbours, features, conv_weight, cpe_weight, cpe_gain)


def exchange_kernel(
    count_ref,
    outgoing_ref,
    notes_ref,
    moved_ref,
    before_ref,
    after_ref,
    summary_ref,
    arrived_ref,
    heard_ref,
    wide_ref,
    tail_ref,
    index_ref,
    order_ref,
    send_sem,
    recv_sem,
    note_send_sem,
    note_recv_sem,
    side_send_sem,
    side_recv_sem,
    local_sem,
):
    devices = outgoing_ref.shape[0]
    across = lax.axis_size("gy")
    me = lax.axis_index("gx") * across + lax.axis_index("gy")

    def place_of(device):
        return (device // across, device % across)

    def to_peer(source, sink, sems, device):
        return pltpu.make_async_remote_copy(
            src_ref=source,
            dst_ref=sink,
            send_sem=sems[0],
            recv_sem=sems[1],
            device_id=place_of(device),
            device_id_type=pl.DeviceIdType.MESH,
        )

    block_sems = (send_sem, recv_sem)
    note_sems = (note_send_sem, note_recv_sem)

    barrier = pltpu.get_barrier_semaphore()

    def greet(step, _):
        peer = place_of((me + step) % devices)
        pl.semaphore_signal(
            barrier, inc=1, device_id=peer, device_id_type=pl.DeviceIdType.MESH
        )
        return 0

    lax.fori_loop(1, devices, greet, 0)
    pl.semaphore_wait(barrier, devices - 1)

    def send(step, _):
        peer = (me + step) % devices
        to_peer(notes_ref.at[peer], heard_ref.at[me], note_sems, peer).start()
        to_peer(outgoing_ref.at[peer], arrived_ref.at[me], block_sems, peer).start()
        return 0

    lax.fori_loop(1, devices, send, 0)
    arrived_ref[me] = outgoing_ref[me]
    heard_ref[me] = notes_ref[me]
    others = pl.ds(0, devices - 1)
    all_notes = to_peer(notes_ref.at[others], heard_ref.at[others], note_sems, me)
    all_notes.wait_recv()

    heard = heard_ref[...].reshape(devices, LANES)
    source = lax.broadcasted_iota(jnp.int32, (devices, LANES), 0)
    lane = lax.broadcasted_iota(jnp.int32, (devices, LANES), 1)
    slots = heard[:, :1]
    index_ref[...] = jnp.max(jnp.where(slots == lane, source, 0), axis=0, keepdims=True)
    counts = heard[:, 1:2]
    offset = jnp.sum(jnp.where(source < me, counts, 0), axis=0, keepdims=True)
    rest = jnp.sum(jnp.where(source < me, 0, counts), axis=0, keepdims=True)
    summary_ref[...] = jnp.where(lane[:1] == 0, offset, rest)
    order = pltpu.make_async_copy(index_ref, order_ref, local_sem)
    order.start()
    order.wait()

    all_blocks = to_peer(outgoing_ref.at[others], arrived_ref.at[others], block_sems, me)
    all_blocks.wait_recv()

    def settle(slot, _):
        block = arrived_ref[order_ref[0, slot]]
        row = pl.multiple_of(slot * BLOCK, BLOCK)
        moved_ref[pl.ds(row, BLOCK), :] = block
        put(wide_ref, row, block.astype(jnp.float32))
        return 0

    lax.fori_loop(0, devices, settle, 0)
    following = (me + 1) % devices
    previous = (me + devices - 1) % devices
    head_sems = (side_send_sem.at[0], side_recv_sem.at[0])
    tail_sems = (side_send_sem.at[1], side_recv_sem.at[1])
    head = to_peer(moved_ref.at[pl.ds(0, PATCH)], after_ref, head_sems, previous)
    head.start()
    start = jnp.clip(count_ref[0] - PATCH, 0, moved_ref.shape[0] - PATCH)
    for part in range(PATCH // QTILE):
        piece = get(wide_ref, start + part * QTILE, QTILE)
        tail_ref[part * QTILE : (part + 1) * QTILE, :] = piece.astype(jnp.bfloat16)
    tail = to_peer(tail_ref, before_ref, tail_sems, following)
    tail.start()
    all_notes.wait_send()
    all_blocks.wait_send()
    head.wait()
    tail.wait()


def exchanged(count, outgoing, notes):
    blocks, block, width = outgoing.shape
    rows = blocks * block
    vmem = pl.BlockSpec(memory_space=pltpu.VMEM)
    smem = pl.BlockSpec(memory_space=pltpu.SMEM)
    side = jax.ShapeDtypeStruct((PATCH, width), jnp.bfloat16)
    dma = pltpu.SemaphoreType.DMA
    return pl.pallas_call(
        exchange_kernel,
        out_shape=(
            jax.ShapeDtypeStruct((rows, width), jnp.bfloat16),
            side,
            side,
            jax.ShapeDtypeStruct((1, LANES), jnp.int32),
        ),
        in_specs=[smem, vmem, vmem],
        out_specs=(vmem, vmem, vmem, vmem),
        scratch_shapes=[
            pltpu.VMEM((blocks, block, width), jnp.bfloat16),
            pltpu.VMEM((blocks, 1, LANES), jnp.int32),
            pltpu.VMEM((width // LANES, rows, LANES), jnp.float32),
            pltpu.VMEM((PATCH, width), jnp.bfloat16),
            pltpu.VMEM((1, LANES), jnp.int32),
            pltpu.SMEM((1, LANES), jnp.int32),
            dma,
            dma,
            dma,
            dma,
            dma((2,)),
            dma((2,)),
            dma,
        ],
        compiler_params=pltpu.CompilerParams(
            vmem_limit_bytes=32 << 20, has_side_effects=True, collective_id=0
        ),
        name="exchange",
    )(count, outgoing, notes)


def block_kernel(
    summary_ref,
    count_ref,
    moved_ref,
    tail_ref,
    head_ref,
    gain_one_ref,
    qkv_ref,
    proj_ref,
    gain_two_ref,
    fc_one_ref,
    fc_two_ref,
    out_ref,
    source_ref,
    own_ref,
    keys_ref,
    values_ref,
    result_ref,
    gathered_ref,
    reach_ref,
    size_ref,
):
    rows, width = moved_ref.shape
    skew = summary_ref[0, 0] % PATCH
    live = count_ref[0]
    known = summary_ref[0, 1] + skew
    live_end = skew + live

    for part in range(PATCH // QTILE):
        piece = tail_ref[part * QTILE : (part + 1) * QTILE, :].astype(jnp.float32)
        put(source_ref, skew + part * QTILE, piece)
    for part in range(rows // QTILE):
        piece = moved_ref[part * QTILE : (part + 1) * QTILE, :].astype(jnp.float32)
        put(source_ref, PATCH + skew + part * QTILE, piece)
        put(own_ref, skew + part * QTILE, piece)
    for part in range(PATCH // QTILE):
        piece = head_ref[part * QTILE : (part + 1) * QTILE, :].astype(jnp.float32)
        put(source_ref, PATCH + live_end + part * QTILE, piece)

    head_of_lane = lax.broadcasted_iota(jnp.int32, (QTILE, width), 1) // (width // HEADS)
    left = lax.broadcasted_iota(jnp.int32, (width, width), 0) // (width // HEADS)
    right = lax.broadcasted_iota(jnp.int32, (width, width), 1) // (width // HEADS)
    same_head = jnp.where(left == right, 1.0, 0.0).astype(jnp.bfloat16)

    def squares(values):
        values = values.astype(jnp.float32)
        total = jnp.dot(
            (values * values).astype(jnp.bfloat16), same_head, preferred_element_type=jnp.float32
        )
        return 1.02 * total

    per_patch = PATCH // QTILE
    patches = (live_end + PATCH - 1) // PATCH

    @pl.loop(0, patches)
    def _(patch):
        for part in range(per_patch):
            start = pl.multiple_of(PATCH + patch * PATCH + part * QTILE, QTILE)
            normed = normalised(get(source_ref, start, QTILE), gain_one_ref[...])
            pair = jnp.dot(
                normed.astype(jnp.bfloat16),
                qkv_ref[:, width:],
                preferred_element_type=jnp.float32,
            )
            columns = slice(part * QTILE, (part + 1) * QTILE)
            some_keys = pair[:, :width].astype(jnp.bfloat16).astype(jnp.float32)
            keys_ref[patch, :, columns] = some_keys.T.astype(jnp.bfloat16)
            alive = start - PATCH + lax.broadcasted_iota(jnp.int32, (QTILE, 1), 0) < known
            some_values = pair[:, width:].astype(jnp.bfloat16)
            for odd in range(2):
                fitted = jnp.where(head_of_lane % 2 == odd, some_values, jnp.bfloat16(1))
                values_ref[patch, odd, columns, :] = jnp.where(alive, fitted, jnp.bfloat16(0))
            reach = jnp.max(squares(some_keys), axis=0, keepdims=True)
            size = jnp.max(jnp.abs(pair[:, width:]), axis=0, keepdims=True)
            reach_ref[patch] = reach if part == 0 else jnp.maximum(reach_ref[patch], reach)
            size_ref[patch] = size if part == 0 else jnp.maximum(size_ref[patch], size)


    def finish(start):
        spots = start + lax.broadcasted_iota(jnp.int32, (QTILE, 1), 0)
        attended = jnp.where(spots < live_end, gathered_ref[...], 0.0)
        projected = jnp.dot(
            attended.astype(jnp.bfloat16), proj_ref[...], preferred_element_type=jnp.float32
        )
        mixed = (get(own_ref, start, QTILE) + projected).astype(jnp.bfloat16).astype(jnp.float32)
        normed = normalised(mixed, gain_two_ref[...]).astype(jnp.bfloat16)
        hidden = jnp.dot(normed, fc_one_ref[...], preferred_element_type=jnp.float32)
        hidden = 0.5 * hidden * (1.0 + lax.erf(hidden * 0.5**0.5))
        final = mixed + jnp.dot(
            hidden.astype(jnp.bfloat16), fc_two_ref[...], preferred_element_type=jnp.float32
        )
        put(result_ref, start, final)

    first_tile = skew // QTILE
    live_tiles = (live_end + QTILE - 1) // QTILE
    all_tiles = (skew + rows + QTILE - 1) // QTILE

    @pl.loop(first_tile, live_tiles)
    def _(tile):
        start = pl.multiple_of(tile * QTILE, QTILE)
        before = pl.multiple_of(jnp.maximum(tile - 1, 0) * QTILE, QTILE)
        patch = tile // per_patch
        normed = normalised(get(own_ref, start, QTILE), gain_one_ref[...]).astype(jnp.bfloat16)
        queries = jnp.dot(normed, qkv_ref[:, :width], preferred_element_type=jnp.float32)
        queries = queries.astype(jnp.bfloat16) * jnp.bfloat16((width // HEADS) ** -0.5)
        reach = jnp.max(squares(queries) * reach_ref[patch])
        safe = (reach <= SAFE_SCORE**2) & (jnp.max(size_ref[patch]) <= SAFE_VALUE)

        def gather(group, odd, softened, so_far):
            heads = [2 * (group * STACK + index) + odd for index in range(STACK)]
            one = jnp.concatenate(
                [jnp.where(head_of_lane == head, queries, jnp.bfloat16(0)) for head in heads],
                axis=0,
            )
            scores = jnp.dot(one, keys_ref[patch], preferred_element_type=jnp.float32)
            grown = softened(scores).astype(jnp.bfloat16)
            mixed = jnp.dot(grown, values_ref[patch, odd], preferred_element_type=jnp.float32)
            spare = LANES - 1 if odd == 0 else 0
            mixed = mixed * (1.0 / mixed[:, spare : spare + 1])
            for index, head in enumerate(heads):
                piece = mixed[index * QTILE : (index + 1) * QTILE]
                so_far = jnp.where(head_of_lane == head, piece, so_far)
            return so_far

        @pl.when(safe)
        def _():
            finish(before)
            so_far = jnp.zeros((QTILE, width), jnp.float32)
            for group in range(HEADS // (2 * STACK)):
                for odd in range(2):
                    so_far = gather(group, odd, jnp.exp, so_far)
            gathered_ref[...] = so_far

        @pl.when(jnp.logical_not(safe))
        def _():
            finish(before)
            spot = patch * PATCH + lax.broadcasted_iota(jnp.int32, (1, PATCH), 1)
            bias = jnp.where(spot < known, 0.0, -1e30)

            def softened(scores):
                scores = scores + bias
                return jnp.exp(scores - jnp.max(scores, axis=-1, keepdims=True))

            @pl.loop(0, HEADS // (2 * STACK))
            def _(group):
                for odd in range(2):
                    gathered_ref[...] = gather(group, odd, softened, gathered_ref[...])

    @pl.loop(live_tiles - 1, all_tiles)
    def _(tile):
        finish(pl.multiple_of(tile * QTILE, QTILE))
        gathered_ref[...] = jnp.zeros((QTILE, width), jnp.float32)

    for part in range(rows // QTILE):
        out_ref[part * QTILE : (part + 1) * QTILE, :] = get(
            result_ref, skew + part * QTILE, QTILE
        ).astype(jnp.bfloat16)


def finished(summary, count, moved, tail, head, gain_one, qkv, proj, gain_two, fc_one, fc_two):
    rows, width = moved.shape
    vmem = pl.BlockSpec(memory_space=pltpu.VMEM)
    smem = pl.BlockSpec(memory_space=pltpu.SMEM)
    most = rows // PATCH + 1
    halves = width // LANES
    return pl.pallas_call(
        block_kernel,
        out_shape=jax.ShapeDtypeStruct((rows, width), jnp.bfloat16),
        in_specs=[smem, smem] + [vmem] * 9,
        out_specs=vmem,
        scratch_shapes=[
            pltpu.VMEM((halves, (most + 2) * PATCH, LANES), jnp.float32),
            pltpu.VMEM((halves, most * PATCH, LANES), jnp.float32),
            pltpu.VMEM((most, width, PATCH), jnp.bfloat16),
            pltpu.VMEM((most, 2, PATCH, width), jnp.bfloat16),
            pltpu.VMEM((halves, most * PATCH, LANES), jnp.float32),
            pltpu.VMEM((QTILE, width), jnp.float32),
            pltpu.VMEM((most, 1, width), jnp.float32),
            pltpu.VMEM((most, 1, width), jnp.float32),
        ],
        compiler_params=pltpu.CompilerParams(vmem_limit_bytes=36 << 20),
        name="attend",
    )(summary, count, moved, tail, head, gain_one, qkv, proj, gain_two, fc_one, fc_two)


def per_device(
    features,
    neighbours,
    counts,
    block_dest,
    conv_weight,
    cpe_weight,
    cpe_gain,
    norm1_gain,
    qkv_weight,
    proj_weight,
    norm2_gain,
    fc1_weight,
    fc2_weight,
):
    rows, width = features.shape[2:]
    taps = neighbours.shape[2]
    own_count = counts.reshape(1)
    outgoing, notes = convolved(
        features.reshape(rows, width),
        neighbours.reshape(taps, rows),
        block_dest.reshape(-1),
        own_count,
        conv_weight.reshape(taps * width, width),
        cpe_weight,
        cpe_gain.reshape(1, width),
    )
    moved, before, after, summary = exchanged(own_count, outgoing, notes)
    block_out = finished(
        summary,
        own_count,
        moved,
        before,
        after,
        norm1_gain.reshape(1, width),
        qkv_weight,
        proj_weight,
        norm2_gain.reshape(1, width),
        fc1_weight,
        fc2_weight,
    )
    return block_out.reshape(1, 1, rows, width)


def solution(mesh):
    placed = (
        P("gx", "gy", None, None),
        P("gx", "gy", None, None),
        P("gx", "gy"),
        P("gx", "gy", None),
    ) + (P(),) * 9
    return jax.shard_map(
        per_device, mesh=mesh, in_specs=placed, out_specs=P("gx", "gy", None, None), check_vma=False
    )
```

```python
import functools

import jax
import jax.numpy as jnp
from jax import lax
from jax.experimental import pallas as pl
from jax.experimental.pallas import tpu as pltpu
from jax.sharding import PartitionSpec as P

HEADS = 16
PATCH = 1024
BLOCK = 16
SUPER = 1024
TILE = 128
WINDOW = 256
QTILE = 256
LANES = 128
STACK = 2
SAFE_SCORE = 30.0
SAFE_VALUE = 1e20


def normalised(values, gain):
    centre = values - jnp.mean(values, axis=-1, keepdims=True)
    spread = jnp.mean(centre * centre, axis=-1, keepdims=True)
    return centre * lax.rsqrt(spread + 1e-05) * gain


def put(ref, start, value):
    for half in range(ref.shape[0]):
        ref[half, pl.ds(start, value.shape[0]), :] = value[:, half * LANES : (half + 1) * LANES]


def get(ref, start, size):
    return jnp.concatenate([ref[half, pl.ds(start, size), :] for half in range(ref.shape[0])], axis=1)


def conv_kernel(
    dest_ref,
    count_ref,
    taps_ref,
    rows_ref,
    weight_ref,
    out_ref,
    own_ref,
    notes_ref,
    picked_ref,
    columns_ref,
    lows_ref,
    passes_ref,
    held_ref,
    held_sem,
):
    taps, tiles, _ = taps_ref.shape
    span = tiles * TILE
    total, width = rows_ref.shape
    blocks = out_ref.shape[0]
    step = pl.program_id(0)
    fetch = pltpu.make_async_copy(weight_ref, held_ref, held_sem)

    @pl.when(step == 0)
    def _():
        fetch.start()

    note_lane = lax.broadcasted_iota(jnp.int32, (1, LANES), 1)
    lanes = lax.broadcasted_iota(jnp.int32, (TILE, WINDOW), 1)

    def columns_of(part):
        chunk = taps_ref[:, part, :]
        spare = jnp.full((-taps % 8, TILE), total, jnp.int32)
        return chunk, jnp.concatenate([chunk, spare], axis=0).T

    def reach(chunk):
        as_float = chunk.astype(jnp.float32)
        low = jnp.min(as_float).astype(jnp.int32) // BLOCK * BLOCK
        high = jnp.max(jnp.where(chunk < total, as_float, -1.0)).astype(jnp.int32)
        passes = (high - low + WINDOW) // WINDOW
        return jnp.minimum(low, total - passes * WINDOW), passes

    def pick(columns, start):
        window = rows_ref[pl.ds(pl.multiple_of(start, BLOCK), WINDOW), :]
        shifted = columns - start
        return [
            jnp.dot(
                jnp.where(shifted[:, tap : tap + 1] == lanes, 1.0, 0.0).astype(jnp.bfloat16),
                window,
                preferred_element_type=jnp.float32,
            ).astype(jnp.bfloat16)
            for tap in range(taps)
        ]

    parts = [columns_of(part) for part in range(span // TILE)]
    ranges = [reach(chunk) for chunk, _ in parts]
    for part, (low, passes) in enumerate(ranges):
        first = pick(parts[part][1], low)
        for tap in range(taps):
            picked_ref[part * TILE : (part + 1) * TILE, tap * width : (tap + 1) * width] = first[tap]
        lows_ref[part] = low
        passes_ref[part] = passes

    @pl.when(functools.reduce(jnp.maximum, [passes for _, passes in ranges]) > 1)
    def _():
        for part in range(span // TILE):
            columns_ref[part] = parts[part][1]

        @pl.loop(0, span // TILE)
        def _(part):
            here = pl.ds(pl.multiple_of(part * TILE, TILE), TILE)

            @pl.loop(1, passes_ref[part])
            def _(index):
                more = pick(columns_ref[part], lows_ref[part] + index * WINDOW)
                for tap in range(taps):
                    columns = slice(tap * width, (tap + 1) * width)
                    picked_ref[here, columns] += more[tap]

    @pl.when(step == 0)
    def _():
        fetch.wait()

    summed = jnp.dot(picked_ref[...], held_ref[...], preferred_element_type=jnp.float32)
    summed = summed.astype(jnp.bfloat16)
    own = rows_ref[pl.ds(pl.multiple_of(step * span, span), span), :]
    for block in range(span // BLOCK):
        place = dest_ref[step * (span // BLOCK) + block]
        target, slot = place // blocks, place % blocks
        out_ref[target] = summed[block * BLOCK : (block + 1) * BLOCK]
        own_ref[target] = own[block * BLOCK : (block + 1) * BLOCK]
        notes_ref[target] = jnp.where(note_lane == 0, slot, count_ref[0])


def convolved(features, neighbours, dest, count, conv_weight):
    total, width = features.shape
    taps = neighbours.shape[0]
    shape = jax.ShapeDtypeStruct((total // BLOCK, BLOCK, width), jnp.bfloat16)
    blocks = total // BLOCK
    whole = lambda step, *_: (0, 0)
    return pl.pallas_call(
        conv_kernel,
        out_shape=(
            shape,
            shape,
            jax.ShapeDtypeStruct((blocks, 1, LANES), jnp.int32),
        ),
        grid_spec=pltpu.PrefetchScalarGridSpec(
            num_scalar_prefetch=2,
            grid=(total // SUPER,),
            in_specs=[
                pl.BlockSpec((taps, SUPER // TILE, TILE), lambda step, *_: (0, step, 0)),
                pl.BlockSpec((total, width), whole),
                pl.BlockSpec(memory_space=pltpu.HBM),
            ],
            out_specs=(
                pl.BlockSpec((blocks, BLOCK, width), lambda step, *_: (0, 0, 0)),
                pl.BlockSpec((blocks, BLOCK, width), lambda step, *_: (0, 0, 0)),
                pl.BlockSpec((blocks, 1, LANES), lambda step, *_: (0, 0, 0)),
            ),
            scratch_shapes=[
                pltpu.VMEM((SUPER, taps * width), jnp.bfloat16),
                pltpu.VMEM((SUPER // TILE, TILE, taps + -taps % 8), jnp.int32),
                pltpu.SMEM((SUPER // TILE,), jnp.int32),
                pltpu.SMEM((SUPER // TILE,), jnp.int32),
                pltpu.VMEM((taps * width, width), jnp.bfloat16),
                pltpu.SemaphoreType.DMA,
            ],
        ),
        compiler_params=pltpu.CompilerParams(vmem_limit_bytes=40 << 20),
        name="convolve",
    )(dest, count, neighbours, features, conv_weight)


def exchange_kernel(
    count_ref,
    summed_ref,
    own_ref,
    notes_ref,
    cpe_ref,
    cpe_gain_ref,
    gain_ref,
    moved_ref,
    normed_ref,
    before_ref,
    after_ref,
    summary_ref,
    outgoing_ref,
    arrived_ref,
    heard_ref,
    wide_ref,
    tail_ref,
    index_ref,
    order_ref,
    send_sem,
    recv_sem,
    note_send_sem,
    note_recv_sem,
    side_send_sem,
    side_recv_sem,
    local_sem,
):
    devices = outgoing_ref.shape[0]
    across = lax.axis_size("gy")
    me = lax.axis_index("gx") * across + lax.axis_index("gy")

    def place_of(device):
        return (device // across, device % across)

    def to_peer(source, sink, sems, device):
        return pltpu.make_async_remote_copy(
            src_ref=source,
            dst_ref=sink,
            send_sem=sems[0],
            recv_sem=sems[1],
            device_id=place_of(device),
            device_id_type=pl.DeviceIdType.MESH,
        )

    block_sems = (send_sem, recv_sem)
    note_sems = (note_send_sem, note_recv_sem)

    barrier = pltpu.get_barrier_semaphore()

    def greet(step, _):
        peer = place_of((me + step) % devices)
        pl.semaphore_signal(
            barrier, inc=1, device_id=peer, device_id_type=pl.DeviceIdType.MESH
        )
        return 0

    lax.fori_loop(1, devices, greet, 0)

    def encode(part, _):
        here = pl.ds(part * (QTILE // BLOCK), QTILE // BLOCK)
        linear = jnp.dot(
            summed_ref[here].reshape(QTILE, -1), cpe_ref[...], preferred_element_type=jnp.float32
        )
        own = own_ref[here].reshape(QTILE, -1).astype(jnp.float32)
        encoded = (own + normalised(linear, cpe_gain_ref[...])).astype(jnp.bfloat16)
        outgoing_ref[here] = encoded.reshape(QTILE // BLOCK, BLOCK, -1)
        return 0

    lax.fori_loop(0, devices * BLOCK // QTILE, encode, 0)
    pl.semaphore_wait(barrier, devices - 1)

    def send(step, _):
        peer = (me + step) % devices
        to_peer(notes_ref.at[peer], heard_ref.at[me], note_sems, peer).start()
        to_peer(outgoing_ref.at[peer], arrived_ref.at[me], block_sems, peer).start()
        return 0

    lax.fori_loop(1, devices, send, 0)
    arrived_ref[me] = outgoing_ref[me]
    heard_ref[me] = notes_ref[me]
    others = pl.ds(0, devices - 1)
    all_notes = to_peer(notes_ref.at[others], heard_ref.at[others], note_sems, me)
    all_notes.wait_recv()

    heard = heard_ref[...].reshape(devices, LANES)
    source = lax.broadcasted_iota(jnp.int32, (devices, LANES), 0)
    lane = lax.broadcasted_iota(jnp.int32, (devices, LANES), 1)
    slots = heard[:, :1]
    index_ref[...] = jnp.max(jnp.where(slots == lane, source, 0), axis=0, keepdims=True)
    counts = heard[:, 1:2]
    offset = jnp.sum(jnp.where(source < me, counts, 0), axis=0, keepdims=True)
    rest = jnp.sum(jnp.where(source < me, 0, counts), axis=0, keepdims=True)
    summary_ref[...] = jnp.where(lane[:1] == 0, offset, rest)
    order = pltpu.make_async_copy(index_ref, order_ref, local_sem)
    order.start()
    order.wait()

    all_blocks = to_peer(outgoing_ref.at[others], arrived_ref.at[others], block_sems, me)
    all_blocks.wait_recv()

    def settle(slot, _):
        block = arrived_ref[order_ref[0, slot]]
        row = pl.multiple_of(slot * BLOCK, BLOCK)
        moved_ref[pl.ds(row, BLOCK), :] = block
        return 0

    lax.fori_loop(0, devices, settle, 0)
    following = (me + 1) % devices
    previous = (me + devices - 1) % devices
    head_sems = (side_send_sem.at[0], side_recv_sem.at[0])
    tail_sems = (side_send_sem.at[1], side_recv_sem.at[1])
    head = to_peer(normed_ref.at[pl.ds(0, PATCH)], after_ref, head_sems, previous)
    for part in range(moved_ref.shape[0] // QTILE):
        here = slice(part * QTILE, (part + 1) * QTILE)
        normed = normalised(moved_ref[here, :].astype(jnp.float32), gain_ref[...])
        normed = normed.astype(jnp.bfloat16)
        normed_ref[here, :] = normed
        put(wide_ref, part * QTILE, normed.astype(jnp.float32))
        if (part + 1) * QTILE == PATCH:
            head.start()
    start = jnp.clip(count_ref[0] - PATCH, 0, moved_ref.shape[0] - PATCH)
    for part in range(PATCH // QTILE):
        piece = get(wide_ref, start + part * QTILE, QTILE)
        tail_ref[part * QTILE : (part + 1) * QTILE, :] = piece.astype(jnp.bfloat16)
    tail = to_peer(tail_ref, before_ref, tail_sems, following)
    tail.start()
    all_notes.wait_send()
    all_blocks.wait_send()
    head.wait()
    tail.wait()


def exchanged(count, summed, own, notes, cpe_weight, cpe_gain, gain):
    blocks, block, width = summed.shape
    rows = blocks * block
    vmem = pl.BlockSpec(memory_space=pltpu.VMEM)
    smem = pl.BlockSpec(memory_space=pltpu.SMEM)
    whole = jax.ShapeDtypeStruct((rows, width), jnp.bfloat16)
    side = jax.ShapeDtypeStruct((PATCH, width), jnp.bfloat16)
    dma = pltpu.SemaphoreType.DMA
    return pl.pallas_call(
        exchange_kernel,
        out_shape=(
            whole,
            whole,
            side,
            side,
            jax.ShapeDtypeStruct((1, LANES), jnp.int32),
        ),
        in_specs=[smem] + [vmem] * 6,
        out_specs=(vmem,) * 5,
        scratch_shapes=[
            pltpu.VMEM((blocks, block, width), jnp.bfloat16),
            pltpu.VMEM((blocks, block, width), jnp.bfloat16),
            pltpu.VMEM((blocks, 1, LANES), jnp.int32),
            pltpu.VMEM((width // LANES, rows, LANES), jnp.float32),
            pltpu.VMEM((PATCH, width), jnp.bfloat16),
            pltpu.VMEM((1, LANES), jnp.int32),
            pltpu.SMEM((1, LANES), jnp.int32),
            dma,
            dma,
            dma,
            dma,
            dma((2,)),
            dma((2,)),
            dma,
        ],
        compiler_params=pltpu.CompilerParams(
            vmem_limit_bytes=32 << 20, has_side_effects=True, collective_id=0
        ),
        name="exchange",
    )(count, summed, own, notes, cpe_weight, cpe_gain, gain)


def block_kernel(
    summary_ref,
    count_ref,
    moved_ref,
    normed_ref,
    tail_ref,
    head_ref,
    qkv_ref,
    proj_ref,
    gain_two_ref,
    fc_one_ref,
    fc_two_ref,
    out_ref,
    source_ref,
    own_ref,
    keys_ref,
    values_ref,
    result_ref,
    gathered_ref,
    reach_ref,
    size_ref,
):
    rows, width = moved_ref.shape
    skew = summary_ref[0, 0] % PATCH
    live = count_ref[0]
    known = summary_ref[0, 1] + skew
    live_end = skew + live

    for part in range(PATCH // QTILE):
        piece = tail_ref[part * QTILE : (part + 1) * QTILE, :].astype(jnp.float32)
        put(source_ref, skew + part * QTILE, piece)
    for part in range(rows // QTILE):
        piece = moved_ref[part * QTILE : (part + 1) * QTILE, :].astype(jnp.float32)
        put(own_ref, skew + part * QTILE, piece)
        piece = normed_ref[part * QTILE : (part + 1) * QTILE, :].astype(jnp.float32)
        put(source_ref, PATCH + skew + part * QTILE, piece)
    for part in range(PATCH // QTILE):
        piece = head_ref[part * QTILE : (part + 1) * QTILE, :].astype(jnp.float32)
        put(source_ref, PATCH + live_end + part * QTILE, piece)

    head_of_lane = lax.broadcasted_iota(jnp.int32, (QTILE, width), 1) // (width // HEADS)
    left = lax.broadcasted_iota(jnp.int32, (width, width), 0) // (width // HEADS)
    right = lax.broadcasted_iota(jnp.int32, (width, width), 1) // (width // HEADS)
    same_head = jnp.where(left == right, 1.0, 0.0).astype(jnp.bfloat16)

    def squares(values):
        values = values.astype(jnp.float32)
        total = jnp.dot(
            (values * values).astype(jnp.bfloat16), same_head, preferred_element_type=jnp.float32
        )
        return 1.02 * total

    per_patch = PATCH // QTILE
    patches = (live_end + PATCH - 1) // PATCH

    @pl.loop(0, patches)
    def _(patch):
        for part in range(per_patch):
            start = pl.multiple_of(PATCH + patch * PATCH + part * QTILE, QTILE)
            pair = jnp.dot(
                get(source_ref, start, QTILE).astype(jnp.bfloat16),
                qkv_ref[:, width:],
                preferred_element_type=jnp.float32,
            )
            columns = slice(part * QTILE, (part + 1) * QTILE)
            some_keys = pair[:, :width].astype(jnp.bfloat16).astype(jnp.float32)
            keys_ref[patch, :, columns] = some_keys.T.astype(jnp.bfloat16)
            alive = start - PATCH + lax.broadcasted_iota(jnp.int32, (QTILE, 1), 0) < known
            some_values = pair[:, width:].astype(jnp.bfloat16)
            for odd in range(2):
                fitted = jnp.where(head_of_lane % 2 == odd, some_values, jnp.bfloat16(1))
                values_ref[patch, odd, columns, :] = jnp.where(alive, fitted, jnp.bfloat16(0))
            reach = jnp.max(squares(some_keys), axis=0, keepdims=True)
            size = jnp.max(jnp.abs(pair[:, width:]), axis=0, keepdims=True)
            reach_ref[patch] = reach if part == 0 else jnp.maximum(reach_ref[patch], reach)
            size_ref[patch] = size if part == 0 else jnp.maximum(size_ref[patch], size)


    def finish(start):
        spots = start + lax.broadcasted_iota(jnp.int32, (QTILE, 1), 0)
        attended = jnp.where(spots < live_end, gathered_ref[...], 0.0)
        projected = jnp.dot(
            attended.astype(jnp.bfloat16), proj_ref[...], preferred_element_type=jnp.float32
        )
        mixed = (get(own_ref, start, QTILE) + projected).astype(jnp.bfloat16).astype(jnp.float32)
        normed = normalised(mixed, gain_two_ref[...]).astype(jnp.bfloat16)
        hidden = jnp.dot(normed, fc_one_ref[...], preferred_element_type=jnp.float32)
        hidden = 0.5 * hidden * (1.0 + lax.erf(hidden * 0.5**0.5))
        final = mixed + jnp.dot(
            hidden.astype(jnp.bfloat16), fc_two_ref[...], preferred_element_type=jnp.float32
        )
        put(result_ref, start, final)

    first_tile = skew // QTILE
    live_tiles = (live_end + QTILE - 1) // QTILE
    all_tiles = (skew + rows + QTILE - 1) // QTILE

    @pl.loop(first_tile, live_tiles)
    def _(tile):
        start = pl.multiple_of(tile * QTILE, QTILE)
        before = pl.multiple_of(jnp.maximum(tile - 1, 0) * QTILE, QTILE)
        patch = tile // per_patch
        normed = get(source_ref, pl.multiple_of(PATCH + start, QTILE), QTILE).astype(jnp.bfloat16)
        queries = jnp.dot(normed, qkv_ref[:, :width], preferred_element_type=jnp.float32)
        queries = queries.astype(jnp.bfloat16) * jnp.bfloat16((width // HEADS) ** -0.5)
        reach = jnp.max(squares(queries) * reach_ref[patch])
        safe = (reach <= SAFE_SCORE**2) & (jnp.max(size_ref[patch]) <= SAFE_VALUE)

        def gather(group, odd, softened, so_far):
            heads = [2 * (group * STACK + index) + odd for index in range(STACK)]
            one = jnp.concatenate(
                [jnp.where(head_of_lane == head, queries, jnp.bfloat16(0)) for head in heads],
                axis=0,
            )
            scores = jnp.dot(one, keys_ref[patch], preferred_element_type=jnp.float32)
            grown = softened(scores).astype(jnp.bfloat16)
            mixed = jnp.dot(grown, values_ref[patch, odd], preferred_element_type=jnp.float32)
            spare = LANES - 1 if odd == 0 else 0
            mixed = mixed * (1.0 / mixed[:, spare : spare + 1])
            for index, head in enumerate(heads):
                piece = mixed[index * QTILE : (index + 1) * QTILE]
                so_far = jnp.where(head_of_lane == head, piece, so_far)
            return so_far

        @pl.when(safe)
        def _():
            finish(before)
            so_far = jnp.zeros((QTILE, width), jnp.float32)
            for group in range(HEADS // (2 * STACK)):
                for odd in range(2):
                    so_far = gather(group, odd, jnp.exp, so_far)
            gathered_ref[...] = so_far

        @pl.when(jnp.logical_not(safe))
        def _():
            finish(before)
            spot = patch * PATCH + lax.broadcasted_iota(jnp.int32, (1, PATCH), 1)
            bias = jnp.where(spot < known, 0.0, -1e30)

            def softened(scores):
                scores = scores + bias
                return jnp.exp(scores - jnp.max(scores, axis=-1, keepdims=True))

            @pl.loop(0, HEADS // (2 * STACK))
            def _(group):
                for odd in range(2):
                    gathered_ref[...] = gather(group, odd, softened, gathered_ref[...])

    @pl.loop(live_tiles - 1, all_tiles)
    def _(tile):
        finish(pl.multiple_of(tile * QTILE, QTILE))
        gathered_ref[...] = jnp.zeros((QTILE, width), jnp.float32)

    for part in range(rows // QTILE):
        out_ref[part * QTILE : (part + 1) * QTILE, :] = get(
            result_ref, skew + part * QTILE, QTILE
        ).astype(jnp.bfloat16)


def finished(summary, count, moved, normed, tail, head, qkv, proj, gain_two, fc_one, fc_two):
    rows, width = moved.shape
    vmem = pl.BlockSpec(memory_space=pltpu.VMEM)
    smem = pl.BlockSpec(memory_space=pltpu.SMEM)
    most = rows // PATCH + 1
    halves = width // LANES
    return pl.pallas_call(
        block_kernel,
        out_shape=jax.ShapeDtypeStruct((rows, width), jnp.bfloat16),
        in_specs=[smem, smem] + [vmem] * 9,
        out_specs=vmem,
        scratch_shapes=[
            pltpu.VMEM((halves, (most + 2) * PATCH, LANES), jnp.float32),
            pltpu.VMEM((halves, most * PATCH, LANES), jnp.float32),
            pltpu.VMEM((most, width, PATCH), jnp.bfloat16),
            pltpu.VMEM((most, 2, PATCH, width), jnp.bfloat16),
            pltpu.VMEM((halves, most * PATCH, LANES), jnp.float32),
            pltpu.VMEM((QTILE, width), jnp.float32),
            pltpu.VMEM((most, 1, width), jnp.float32),
            pltpu.VMEM((most, 1, width), jnp.float32),
        ],
        compiler_params=pltpu.CompilerParams(vmem_limit_bytes=36 << 20),
        name="attend",
    )(summary, count, moved, normed, tail, head, qkv, proj, gain_two, fc_one, fc_two)


def per_device(
    features,
    neighbours,
    counts,
    block_dest,
    conv_weight,
    cpe_weight,
    cpe_gain,
    norm1_gain,
    qkv_weight,
    proj_weight,
    norm2_gain,
    fc1_weight,
    fc2_weight,
):
    rows, width = features.shape[2:]
    taps = neighbours.shape[2]
    def afar(value):
        return pltpu.with_memory_space_constraint(value, pltpu.HBM)

    own_count = counts.reshape(1)
    summed, own, notes = convolved(
        afar(features.reshape(rows, width)),
        afar(neighbours.reshape(taps, rows // TILE, TILE)),
        afar(block_dest.reshape(-1)),
        own_count,
        afar(conv_weight.reshape(taps * width, width)),
    )
    moved, normed, before, after, summary = exchanged(
        own_count,
        summed,
        own,
        notes,
        cpe_weight,
        cpe_gain.reshape(1, width),
        norm1_gain.reshape(1, width),
    )
    block_out = finished(
        summary,
        own_count,
        moved,
        normed,
        before,
        after,
        qkv_weight,
        proj_weight,
        norm2_gain.reshape(1, width),
        fc1_weight,
        fc2_weight,
    )
    return block_out.reshape(1, 1, rows, width)


def solution(mesh):
    placed = (
        P("gx", "gy", None, None),
        P("gx", "gy", None, None),
        P("gx", "gy"),
        P("gx", "gy", None),
    ) + (P(),) * 9
    return jax.shard_map(
        per_device, mesh=mesh, in_specs=placed, out_specs=P("gx", "gy", None, None), check_vma=False
    )
```

```python
import functools

import jax
import jax.numpy as jnp
from jax import lax
from jax.experimental import pallas as pl
from jax.experimental.pallas import tpu as pltpu
from jax.sharding import PartitionSpec as P

HEADS = 16
PATCH = 1024
BLOCK = 16
SUPER = 1024
TILE = 128
WINDOW = 256
QTILE = 256
LANES = 128
STACK = 2
SAFE_SCORE = 30.0
SAFE_VALUE = 1e20


def normalised(values, gain):
    centre = values - jnp.mean(values, axis=-1, keepdims=True)
    spread = jnp.mean(centre * centre, axis=-1, keepdims=True)
    return centre * lax.rsqrt(spread + 1e-05) * gain


def put(ref, start, value):
    for half in range(ref.shape[0]):
        ref[half, pl.ds(start, value.shape[0]), :] = value[:, half * LANES : (half + 1) * LANES]


def get(ref, start, size):
    return jnp.concatenate([ref[half, pl.ds(start, size), :] for half in range(ref.shape[0])], axis=1)


def conv_kernel(
    dest_ref,
    count_ref,
    taps_ref,
    rows_ref,
    weight_ref,
    out_ref,
    own_ref,
    notes_ref,
    picked_ref,
    columns_ref,
    lows_ref,
    passes_ref,
    held_ref,
    held_sem,
):
    taps, tiles, _ = taps_ref.shape
    span = tiles * TILE
    total, width = rows_ref.shape
    blocks = out_ref.shape[0]
    step = pl.program_id(0)
    fetch = pltpu.make_async_copy(weight_ref, held_ref, held_sem)

    @pl.when(step == 0)
    def _():
        fetch.start()

    note_lane = lax.broadcasted_iota(jnp.int32, (1, LANES), 1)
    lanes = lax.broadcasted_iota(jnp.int32, (TILE, WINDOW), 1)

    def columns_of(part):
        chunk = taps_ref[:, part, :]
        spare = jnp.full((-taps % 8, TILE), total, jnp.int32)
        return chunk, jnp.concatenate([chunk, spare], axis=0).T

    def reach(chunk):
        as_float = chunk.astype(jnp.float32)
        low = jnp.min(as_float).astype(jnp.int32) // BLOCK * BLOCK
        high = jnp.max(jnp.where(chunk < total, as_float, -1.0)).astype(jnp.int32)
        passes = (high - low + WINDOW) // WINDOW
        return jnp.minimum(low, total - passes * WINDOW), passes

    def pick(columns, start):
        window = rows_ref[pl.ds(pl.multiple_of(start, BLOCK), WINDOW), :]
        shifted = columns - start
        return [
            jnp.dot(
                jnp.where(shifted[:, tap : tap + 1] == lanes, 1.0, 0.0).astype(jnp.bfloat16),
                window,
                preferred_element_type=jnp.float32,
            ).astype(jnp.bfloat16)
            for tap in range(taps)
        ]

    parts = [columns_of(part) for part in range(span // TILE)]
    ranges = [reach(chunk) for chunk, _ in parts]
    for part, (low, passes) in enumerate(ranges):
        first = pick(parts[part][1], low)
        for tap in range(taps):
            picked_ref[part * TILE : (part + 1) * TILE, tap * width : (tap + 1) * width] = first[tap]
        lows_ref[part] = low
        passes_ref[part] = passes

    @pl.when(functools.reduce(jnp.maximum, [passes for _, passes in ranges]) > 1)
    def _():
        for part in range(span // TILE):
            columns_ref[part] = parts[part][1]

        @pl.loop(0, span // TILE)
        def _(part):
            here = pl.ds(pl.multiple_of(part * TILE, TILE), TILE)

            @pl.loop(1, passes_ref[part])
            def _(index):
                more = pick(columns_ref[part], lows_ref[part] + index * WINDOW)
                for tap in range(taps):
                    columns = slice(tap * width, (tap + 1) * width)
                    picked_ref[here, columns] += more[tap]

    @pl.when(step == 0)
    def _():
        fetch.wait()

    summed = jnp.dot(picked_ref[...], held_ref[...], preferred_element_type=jnp.float32)
    summed = summed.astype(jnp.bfloat16)
    own = rows_ref[pl.ds(pl.multiple_of(step * span, span), span), :]
    for block in range(span // BLOCK):
        place = dest_ref[step * (span // BLOCK) + block]
        target, slot = place // blocks, place % blocks
        out_ref[target] = summed[block * BLOCK : (block + 1) * BLOCK]
        own_ref[target] = own[block * BLOCK : (block + 1) * BLOCK]
        notes_ref[target] = jnp.where(note_lane == 0, slot, count_ref[0])


def convolved(features, neighbours, dest, count, conv_weight):
    total, width = features.shape
    taps = neighbours.shape[0]
    shape = jax.ShapeDtypeStruct((total // BLOCK, BLOCK, width), jnp.bfloat16)
    blocks = total // BLOCK
    whole = lambda step, *_: (0, 0)
    return pl.pallas_call(
        conv_kernel,
        out_shape=(
            shape,
            shape,
            jax.ShapeDtypeStruct((blocks, 1, LANES), jnp.int32),
        ),
        grid_spec=pltpu.PrefetchScalarGridSpec(
            num_scalar_prefetch=2,
            grid=(total // SUPER,),
            in_specs=[
                pl.BlockSpec((taps, SUPER // TILE, TILE), lambda step, *_: (0, step, 0)),
                pl.BlockSpec((total, width), whole),
                pl.BlockSpec(memory_space=pltpu.HBM),
            ],
            out_specs=(
                pl.BlockSpec((blocks, BLOCK, width), lambda step, *_: (0, 0, 0)),
                pl.BlockSpec((blocks, BLOCK, width), lambda step, *_: (0, 0, 0)),
                pl.BlockSpec((blocks, 1, LANES), lambda step, *_: (0, 0, 0)),
            ),
            scratch_shapes=[
                pltpu.VMEM((SUPER, taps * width), jnp.bfloat16),
                pltpu.VMEM((SUPER // TILE, TILE, taps + -taps % 8), jnp.int32),
                pltpu.SMEM((SUPER // TILE,), jnp.int32),
                pltpu.SMEM((SUPER // TILE,), jnp.int32),
                pltpu.VMEM((taps * width, width), jnp.bfloat16),
                pltpu.SemaphoreType.DMA,
            ],
        ),
        compiler_params=pltpu.CompilerParams(vmem_limit_bytes=40 << 20),
        name="convolve",
    )(dest, count, neighbours, features, conv_weight)


def exchange_kernel(
    count_ref,
    summed_ref,
    own_ref,
    notes_ref,
    cpe_ref,
    cpe_gain_ref,
    gain_ref,
    moved_ref,
    normed_ref,
    before_ref,
    after_ref,
    summary_ref,
    outgoing_ref,
    arrived_ref,
    heard_ref,
    wide_ref,
    tail_ref,
    index_ref,
    order_ref,
    send_sem,
    recv_sem,
    note_send_sem,
    note_recv_sem,
    side_send_sem,
    side_recv_sem,
    local_sem,
):
    devices = outgoing_ref.shape[0]
    across = lax.axis_size("gy")
    me = lax.axis_index("gx") * across + lax.axis_index("gy")

    def place_of(device):
        return (device // across, device % across)

    def to_peer(source, sink, sems, device):
        return pltpu.make_async_remote_copy(
            src_ref=source,
            dst_ref=sink,
            send_sem=sems[0],
            recv_sem=sems[1],
            device_id=place_of(device),
            device_id_type=pl.DeviceIdType.MESH,
        )

    block_sems = (send_sem, recv_sem)
    note_sems = (note_send_sem, note_recv_sem)

    barrier = pltpu.get_barrier_semaphore()

    def greet(step, _):
        peer = place_of((me + step) % devices)
        pl.semaphore_signal(
            barrier, inc=1, device_id=peer, device_id_type=pl.DeviceIdType.MESH
        )
        return 0

    lax.fori_loop(1, devices, greet, 0)

    def encode(part, _):
        here = pl.ds(part * (QTILE // BLOCK), QTILE // BLOCK)
        linear = jnp.dot(
            summed_ref[here].reshape(QTILE, -1), cpe_ref[...], preferred_element_type=jnp.float32
        )
        own = own_ref[here].reshape(QTILE, -1).astype(jnp.float32)
        encoded = (own + normalised(linear, cpe_gain_ref[...])).astype(jnp.bfloat16)
        outgoing_ref[here] = encoded.reshape(QTILE // BLOCK, BLOCK, -1)
        return 0

    lax.fori_loop(0, devices * BLOCK // QTILE, encode, 0)
    pl.semaphore_wait(barrier, devices - 1)

    def send(step, _):
        peer = (me + step) % devices
        to_peer(notes_ref.at[peer], heard_ref.at[me], note_sems, peer).start()
        to_peer(outgoing_ref.at[peer], arrived_ref.at[me], block_sems, peer).start()
        return 0

    lax.fori_loop(1, devices, send, 0)
    arrived_ref[me] = outgoing_ref[me]
    heard_ref[me] = notes_ref[me]
    others = pl.ds(0, devices - 1)
    all_notes = to_peer(notes_ref.at[others], heard_ref.at[others], note_sems, me)
    all_notes.wait_recv()

    heard = heard_ref[...].reshape(devices, LANES)
    source = lax.broadcasted_iota(jnp.int32, (devices, LANES), 0)
    lane = lax.broadcasted_iota(jnp.int32, (devices, LANES), 1)
    slots = heard[:, :1]
    index_ref[...] = jnp.max(jnp.where(slots == lane, source, 0), axis=0, keepdims=True)
    counts = heard[:, 1:2]
    offset = jnp.sum(jnp.where(source < me, counts, 0), axis=0, keepdims=True)
    rest = jnp.sum(jnp.where(source < me, 0, counts), axis=0, keepdims=True)
    summary_ref[...] = jnp.where(lane[:1] == 0, offset, rest)
    order = pltpu.make_async_copy(index_ref, order_ref, local_sem)
    order.start()
    order.wait()

    all_blocks = to_peer(outgoing_ref.at[others], arrived_ref.at[others], block_sems, me)
    all_blocks.wait_recv()

    def settle(slot, _):
        block = arrived_ref[order_ref[0, slot]]
        row = pl.multiple_of(slot * BLOCK, BLOCK)
        moved_ref[pl.ds(row, BLOCK), :] = block
        put(wide_ref, row, block.astype(jnp.float32))
        return 0

    lax.fori_loop(0, devices, settle, 0, unroll=8)
    following = (me + 1) % devices
    previous = (me + devices - 1) % devices
    head_sems = (side_send_sem.at[0], side_recv_sem.at[0])
    tail_sems = (side_send_sem.at[1], side_recv_sem.at[1])
    rows = devices * BLOCK
    head = to_peer(normed_ref.at[pl.ds(0, PATCH)], after_ref, head_sems, previous)
    tail = to_peer(tail_ref, before_ref, tail_sems, following)
    start = jnp.clip(count_ref[0] - PATCH, 0, rows - PATCH)

    def first_norm(first):
        return normalised(get(wide_ref, first, QTILE), gain_ref[...]).astype(jnp.bfloat16)

    for part in range(PATCH // QTILE):
        here = pl.ds(part * QTILE, QTILE)
        tail_ref[here, :] = first_norm(start + part * QTILE)
        to_peer(tail_ref.at[here], before_ref.at[here], tail_sems, following).start()
        normed_ref[here, :] = first_norm(part * QTILE)
        to_peer(normed_ref.at[here], after_ref.at[here], head_sems, previous).start()
    for part in range(PATCH // QTILE, rows // QTILE):
        normed_ref[pl.ds(part * QTILE, QTILE), :] = first_norm(part * QTILE)
    all_notes.wait_send()
    all_blocks.wait_send()
    head.wait()
    tail.wait()


def exchanged(count, summed, own, notes, cpe_weight, cpe_gain, gain):
    blocks, block, width = summed.shape
    rows = blocks * block
    vmem = pl.BlockSpec(memory_space=pltpu.VMEM)
    smem = pl.BlockSpec(memory_space=pltpu.SMEM)
    whole = jax.ShapeDtypeStruct((rows, width), jnp.bfloat16)
    side = jax.ShapeDtypeStruct((PATCH, width), jnp.bfloat16)
    dma = pltpu.SemaphoreType.DMA
    return pl.pallas_call(
        exchange_kernel,
        out_shape=(
            whole,
            whole,
            side,
            side,
            jax.ShapeDtypeStruct((1, LANES), jnp.int32),
        ),
        in_specs=[smem] + [vmem] * 6,
        out_specs=(vmem,) * 5,
        scratch_shapes=[
            pltpu.VMEM((blocks, block, width), jnp.bfloat16),
            pltpu.VMEM((blocks, block, width), jnp.bfloat16),
            pltpu.VMEM((blocks, 1, LANES), jnp.int32),
            pltpu.VMEM((width // LANES, rows, LANES), jnp.float32),
            pltpu.VMEM((PATCH, width), jnp.bfloat16),
            pltpu.VMEM((1, LANES), jnp.int32),
            pltpu.SMEM((1, LANES), jnp.int32),
            dma,
            dma,
            dma,
            dma,
            dma((2,)),
            dma((2,)),
            dma,
        ],
        compiler_params=pltpu.CompilerParams(
            vmem_limit_bytes=32 << 20, has_side_effects=True, collective_id=0
        ),
        name="exchange",
    )(count, summed, own, notes, cpe_weight, cpe_gain, gain)


def block_kernel(
    summary_ref,
    count_ref,
    moved_ref,
    normed_ref,
    tail_ref,
    head_ref,
    qkv_ref,
    proj_ref,
    gain_two_ref,
    fc_one_ref,
    fc_two_ref,
    out_ref,
    source_ref,
    own_ref,
    keys_ref,
    values_ref,
    result_ref,
    gathered_ref,
    reach_ref,
    size_ref,
):
    rows, width = moved_ref.shape
    skew = summary_ref[0, 0] % PATCH
    live = count_ref[0]
    known = summary_ref[0, 1] + skew
    live_end = skew + live

    for part in range(PATCH // QTILE):
        piece = tail_ref[part * QTILE : (part + 1) * QTILE, :].astype(jnp.float32)
        put(source_ref, skew + part * QTILE, piece)
    for part in range(rows // QTILE):
        piece = moved_ref[part * QTILE : (part + 1) * QTILE, :].astype(jnp.float32)
        put(own_ref, skew + part * QTILE, piece)
        piece = normed_ref[part * QTILE : (part + 1) * QTILE, :].astype(jnp.float32)
        put(source_ref, PATCH + skew + part * QTILE, piece)
    for part in range(PATCH // QTILE):
        piece = head_ref[part * QTILE : (part + 1) * QTILE, :].astype(jnp.float32)
        put(source_ref, PATCH + live_end + part * QTILE, piece)

    head_of_lane = lax.broadcasted_iota(jnp.int32, (QTILE, width), 1) // (width // HEADS)
    left = lax.broadcasted_iota(jnp.int32, (width, width), 0) // (width // HEADS)
    right = lax.broadcasted_iota(jnp.int32, (width, width), 1) // (width // HEADS)
    same_head = jnp.where(left == right, 1.0, 0.0).astype(jnp.bfloat16)

    def squares(values):
        values = values.astype(jnp.float32)
        total = jnp.dot(
            (values * values).astype(jnp.bfloat16), same_head, preferred_element_type=jnp.float32
        )
        return 1.02 * total

    per_patch = PATCH // QTILE
    patches = (live_end + PATCH - 1) // PATCH

    @pl.loop(0, patches)
    def _(patch):
        for part in range(per_patch):
            start = pl.multiple_of(PATCH + patch * PATCH + part * QTILE, QTILE)
            pair = jnp.dot(
                get(source_ref, start, QTILE).astype(jnp.bfloat16),
                qkv_ref[:, width:],
                preferred_element_type=jnp.float32,
            )
            columns = slice(part * QTILE, (part + 1) * QTILE)
            some_keys = pair[:, :width].astype(jnp.bfloat16).astype(jnp.float32)
            keys_ref[patch, :, columns] = some_keys.T.astype(jnp.bfloat16)
            alive = start - PATCH + lax.broadcasted_iota(jnp.int32, (QTILE, 1), 0) < known
            some_values = pair[:, width:].astype(jnp.bfloat16)
            for odd in range(2):
                fitted = jnp.where(head_of_lane % 2 == odd, some_values, jnp.bfloat16(1))
                values_ref[patch, odd, columns, :] = jnp.where(alive, fitted, jnp.bfloat16(0))
            reach = jnp.max(squares(some_keys), axis=0, keepdims=True)
            size = jnp.max(jnp.abs(pair[:, width:]), axis=0, keepdims=True)
            reach_ref[patch] = reach if part == 0 else jnp.maximum(reach_ref[patch], reach)
            size_ref[patch] = size if part == 0 else jnp.maximum(size_ref[patch], size)


    def finish(start):
        spots = start + lax.broadcasted_iota(jnp.int32, (QTILE, 1), 0)
        attended = jnp.where(spots < live_end, gathered_ref[...], 0.0)
        projected = jnp.dot(
            attended.astype(jnp.bfloat16), proj_ref[...], preferred_element_type=jnp.float32
        )
        mixed = (get(own_ref, start, QTILE) + projected).astype(jnp.bfloat16).astype(jnp.float32)
        normed = normalised(mixed, gain_two_ref[...]).astype(jnp.bfloat16)
        hidden = jnp.dot(normed, fc_one_ref[...], preferred_element_type=jnp.float32)
        hidden = 0.5 * hidden * (1.0 + lax.erf(hidden * 0.5**0.5))
        final = mixed + jnp.dot(
            hidden.astype(jnp.bfloat16), fc_two_ref[...], preferred_element_type=jnp.float32
        )
        put(result_ref, start, final)

    first_tile = skew // QTILE
    live_tiles = (live_end + QTILE - 1) // QTILE
    all_tiles = (skew + rows + QTILE - 1) // QTILE

    @pl.loop(first_tile, live_tiles)
    def _(tile):
        start = pl.multiple_of(tile * QTILE, QTILE)
        before = pl.multiple_of(jnp.maximum(tile - 1, 0) * QTILE, QTILE)
        patch = tile // per_patch
        normed = get(source_ref, pl.multiple_of(PATCH + start, QTILE), QTILE).astype(jnp.bfloat16)
        queries = jnp.dot(normed, qkv_ref[:, :width], preferred_element_type=jnp.float32)
        queries = queries.astype(jnp.bfloat16) * jnp.bfloat16((width // HEADS) ** -0.5)
        reach = jnp.max(squares(queries) * reach_ref[patch])
        safe = (reach <= SAFE_SCORE**2) & (jnp.max(size_ref[patch]) <= SAFE_VALUE)

        def grow(group, odd, softened):
            heads = [2 * (group * STACK + index) + odd for index in range(STACK)]
            one = jnp.concatenate(
                [jnp.where(head_of_lane == head, queries, jnp.bfloat16(0)) for head in heads],
                axis=0,
            )
            scores = jnp.dot(one, keys_ref[patch], preferred_element_type=jnp.float32)
            return heads, softened(scores).astype(jnp.bfloat16)

        def gather(heads, odd, grown, so_far):
            mixed = jnp.dot(grown, values_ref[patch, odd], preferred_element_type=jnp.float32)
            spare = LANES - 1 if odd == 0 else 0
            mixed = mixed * (1.0 / mixed[:, spare : spare + 1])
            for index, head in enumerate(heads):
                piece = mixed[index * QTILE : (index + 1) * QTILE]
                so_far = jnp.where(head_of_lane == head, piece, so_far)
            return so_far

        @pl.when(safe)
        def _():
            steps = [(group, odd) for group in range(HEADS // (2 * STACK)) for odd in range(2)]
            so_far = jnp.zeros((QTILE, width), jnp.float32)
            ready = [grow(*steps[0], jnp.exp)]
            finish(before)
            for index, (_, odd) in enumerate(steps):
                if index + 1 < len(steps):
                    ready.append(grow(*steps[index + 1], jnp.exp))
                so_far = gather(ready[index][0], odd, ready[index][1], so_far)
            gathered_ref[...] = so_far

        @pl.when(jnp.logical_not(safe))
        def _():
            finish(before)
            spot = patch * PATCH + lax.broadcasted_iota(jnp.int32, (1, PATCH), 1)
            bias = jnp.where(spot < known, 0.0, -1e30)

            def softened(scores):
                scores = scores + bias
                return jnp.exp(scores - jnp.max(scores, axis=-1, keepdims=True))

            @pl.loop(0, HEADS // (2 * STACK))
            def _(group):
                for odd in range(2):
                    heads, grown = grow(group, odd, softened)
                    gathered_ref[...] = gather(heads, odd, grown, gathered_ref[...])

    @pl.loop(live_tiles - 1, all_tiles)
    def _(tile):
        finish(pl.multiple_of(tile * QTILE, QTILE))
        gathered_ref[...] = jnp.zeros((QTILE, width), jnp.float32)

    for part in range(rows // QTILE):
        out_ref[part * QTILE : (part + 1) * QTILE, :] = get(
            result_ref, skew + part * QTILE, QTILE
        ).astype(jnp.bfloat16)


def finished(summary, count, moved, normed, tail, head, qkv, proj, gain_two, fc_one, fc_two):
    rows, width = moved.shape
    vmem = pl.BlockSpec(memory_space=pltpu.VMEM)
    smem = pl.BlockSpec(memory_space=pltpu.SMEM)
    most = rows // PATCH + 1
    halves = width // LANES
    return pl.pallas_call(
        block_kernel,
        out_shape=jax.ShapeDtypeStruct((rows, width), jnp.bfloat16),
        in_specs=[smem, smem] + [vmem] * 9,
        out_specs=vmem,
        scratch_shapes=[
            pltpu.VMEM((halves, (most + 2) * PATCH, LANES), jnp.float32),
            pltpu.VMEM((halves, most * PATCH, LANES), jnp.float32),
            pltpu.VMEM((most, width, PATCH), jnp.bfloat16),
            pltpu.VMEM((most, 2, PATCH, width), jnp.bfloat16),
            pltpu.VMEM((halves, most * PATCH, LANES), jnp.float32),
            pltpu.VMEM((QTILE, width), jnp.float32),
            pltpu.VMEM((most, 1, width), jnp.float32),
            pltpu.VMEM((most, 1, width), jnp.float32),
        ],
        compiler_params=pltpu.CompilerParams(vmem_limit_bytes=36 << 20),
        name="attend",
    )(summary, count, moved, normed, tail, head, qkv, proj, gain_two, fc_one, fc_two)


def per_device(
    features,
    neighbours,
    counts,
    block_dest,
    conv_weight,
    cpe_weight,
    cpe_gain,
    norm1_gain,
    qkv_weight,
    proj_weight,
    norm2_gain,
    fc1_weight,
    fc2_weight,
):
    rows, width = features.shape[2:]
    taps = neighbours.shape[2]
    def afar(value):
        return pltpu.with_memory_space_constraint(value, pltpu.HBM)

    own_count = counts.reshape(1)
    summed, own, notes = convolved(
        afar(features.reshape(rows, width)),
        afar(neighbours.reshape(taps, rows // TILE, TILE)),
        afar(block_dest.reshape(-1)),
        own_count,
        afar(conv_weight.reshape(taps * width, width)),
    )
    moved, normed, before, after, summary = exchanged(
        own_count,
        summed,
        own,
        notes,
        cpe_weight,
        cpe_gain.reshape(1, width),
        norm1_gain.reshape(1, width),
    )
    block_out = finished(
        summary,
        own_count,
        moved,
        normed,
        before,
        after,
        qkv_weight,
        proj_weight,
        norm2_gain.reshape(1, width),
        fc1_weight,
        fc2_weight,
    )
    return block_out.reshape(1, 1, rows, width)


def solution(mesh):
    placed = (
        P("gx", "gy", None, None),
        P("gx", "gy", None, None),
        P("gx", "gy"),
        P("gx", "gy", None),
    ) + (P(),) * 9
    return jax.shard_map(
        per_device, mesh=mesh, in_specs=placed, out_specs=P("gx", "gy", None, None), check_vma=False
    )
```

```python
import functools

import jax
import jax.numpy as jnp
from jax import lax
from jax.experimental import pallas as pl
from jax.experimental.pallas import tpu as pltpu
from jax.sharding import PartitionSpec as P

HEADS = 16
PATCH = 1024
BLOCK = 16
SUPER = 1024
TILE = 128
WINDOW = 256
QTILE = 256
LANES = 128
STACK = 2
SAFE_SCORE = 30.0
SAFE_VALUE = 1e20


def normalised(values, gain):
    centre = values - jnp.mean(values, axis=-1, keepdims=True)
    spread = jnp.mean(centre * centre, axis=-1, keepdims=True)
    return centre * lax.rsqrt(spread + 1e-05) * gain


def put(ref, start, value):
    for half in range(ref.shape[0]):
        ref[half, pl.ds(start, value.shape[0]), :] = value[:, half * LANES : (half + 1) * LANES]


def get(ref, start, size):
    return jnp.concatenate([ref[half, pl.ds(start, size), :] for half in range(ref.shape[0])], axis=1)


def conv_kernel(
    dest_ref,
    count_ref,
    taps_ref,
    rows_ref,
    weight_ref,
    out_ref,
    own_ref,
    notes_ref,
    picked_ref,
    columns_ref,
    lows_ref,
    passes_ref,
    held_ref,
    held_sem,
):
    taps, tiles, _ = taps_ref.shape
    span = tiles * TILE
    total, width = rows_ref.shape
    blocks = out_ref.shape[0]
    step = pl.program_id(0)
    fetch = pltpu.make_async_copy(weight_ref, held_ref, held_sem)

    @pl.when(step == 0)
    def _():
        fetch.start()

    note_lane = lax.broadcasted_iota(jnp.int32, (1, LANES), 1)
    lanes = lax.broadcasted_iota(jnp.int32, (TILE, WINDOW), 1)

    def columns_of(part):
        chunk = taps_ref[:, part, :]
        spare = jnp.full((-taps % 8, TILE), total, jnp.int32)
        return chunk, jnp.concatenate([chunk, spare], axis=0).T

    def reach(chunk):
        as_float = chunk.astype(jnp.float32)
        low = jnp.min(as_float).astype(jnp.int32) // BLOCK * BLOCK
        high = jnp.max(jnp.where(chunk < total, as_float, -1.0)).astype(jnp.int32)
        passes = (high - low + WINDOW) // WINDOW
        return jnp.minimum(low, total - passes * WINDOW), passes

    def pick(columns, start):
        window = rows_ref[pl.ds(pl.multiple_of(start, BLOCK), WINDOW), :]
        shifted = columns - start
        return [
            jnp.dot(
                jnp.where(shifted[:, tap : tap + 1] == lanes, 1.0, 0.0).astype(jnp.bfloat16),
                window,
                preferred_element_type=jnp.float32,
            ).astype(jnp.bfloat16)
            for tap in range(taps)
        ]

    parts = [columns_of(part) for part in range(span // TILE)]
    ranges = [reach(chunk) for chunk, _ in parts]
    for part, (low, passes) in enumerate(ranges):
        first = pick(parts[part][1], low)
        for tap in range(taps):
            picked_ref[part * TILE : (part + 1) * TILE, tap * width : (tap + 1) * width] = first[tap]
        lows_ref[part] = low
        passes_ref[part] = passes

    @pl.when(functools.reduce(jnp.maximum, [passes for _, passes in ranges]) > 1)
    def _():
        for part in range(span // TILE):
            columns_ref[part] = parts[part][1]

        @pl.loop(0, span // TILE)
        def _(part):
            here = pl.ds(pl.multiple_of(part * TILE, TILE), TILE)

            @pl.loop(1, passes_ref[part])
            def _(index):
                more = pick(columns_ref[part], lows_ref[part] + index * WINDOW)
                for tap in range(taps):
                    columns = slice(tap * width, (tap + 1) * width)
                    picked_ref[here, columns] += more[tap]

    @pl.when(step == 0)
    def _():
        fetch.wait()

    summed = jnp.dot(picked_ref[...], held_ref[...], preferred_element_type=jnp.float32)
    summed = summed.astype(jnp.bfloat16)
    own = rows_ref[pl.ds(pl.multiple_of(step * span, span), span), :]
    for block in range(span // BLOCK):
        place = dest_ref[step * (span // BLOCK) + block]
        target, slot = place // blocks, place % blocks
        out_ref[target] = summed[block * BLOCK : (block + 1) * BLOCK]
        own_ref[target] = own[block * BLOCK : (block + 1) * BLOCK]
        notes_ref[target] = jnp.where(note_lane == 0, slot, count_ref[0])


def convolved(features, neighbours, dest, count, conv_weight):
    total, width = features.shape
    taps = neighbours.shape[0]
    shape = jax.ShapeDtypeStruct((total // BLOCK, BLOCK, width), jnp.bfloat16)
    blocks = total // BLOCK
    whole = lambda step, *_: (0, 0)
    return pl.pallas_call(
        conv_kernel,
        out_shape=(
            shape,
            shape,
            jax.ShapeDtypeStruct((blocks, 1, LANES), jnp.int32),
        ),
        grid_spec=pltpu.PrefetchScalarGridSpec(
            num_scalar_prefetch=2,
            grid=(total // SUPER,),
            in_specs=[
                pl.BlockSpec((taps, SUPER // TILE, TILE), lambda step, *_: (0, step, 0)),
                pl.BlockSpec((total, width), whole),
                pl.BlockSpec(memory_space=pltpu.HBM),
            ],
            out_specs=(
                pl.BlockSpec((blocks, BLOCK, width), lambda step, *_: (0, 0, 0)),
                pl.BlockSpec((blocks, BLOCK, width), lambda step, *_: (0, 0, 0)),
                pl.BlockSpec((blocks, 1, LANES), lambda step, *_: (0, 0, 0)),
            ),
            scratch_shapes=[
                pltpu.VMEM((SUPER, taps * width), jnp.bfloat16),
                pltpu.VMEM((SUPER // TILE, TILE, taps + -taps % 8), jnp.int32),
                pltpu.SMEM((SUPER // TILE,), jnp.int32),
                pltpu.SMEM((SUPER // TILE,), jnp.int32),
                pltpu.VMEM((taps * width, width), jnp.bfloat16),
                pltpu.SemaphoreType.DMA,
            ],
        ),
        compiler_params=pltpu.CompilerParams(vmem_limit_bytes=40 << 20),
        name="convolve",
    )(dest, count, neighbours, features, conv_weight)


def exchange_kernel(
    count_ref,
    summed_ref,
    own_ref,
    notes_ref,
    cpe_ref,
    cpe_gain_ref,
    gain_ref,
    moved_ref,
    normed_ref,
    before_ref,
    after_ref,
    summary_ref,
    outgoing_ref,
    arrived_ref,
    heard_ref,
    wide_ref,
    tail_ref,
    index_ref,
    order_ref,
    send_sem,
    recv_sem,
    note_send_sem,
    note_recv_sem,
    side_send_sem,
    side_recv_sem,
    local_sem,
):
    devices = outgoing_ref.shape[0]
    across = lax.axis_size("gy")
    me = lax.axis_index("gx") * across + lax.axis_index("gy")

    def place_of(device):
        return (device // across, device % across)

    def to_peer(source, sink, sems, device):
        return pltpu.make_async_remote_copy(
            src_ref=source,
            dst_ref=sink,
            send_sem=sems[0],
            recv_sem=sems[1],
            device_id=place_of(device),
            device_id_type=pl.DeviceIdType.MESH,
        )

    block_sems = (send_sem, recv_sem)
    note_sems = (note_send_sem, note_recv_sem)

    barrier = pltpu.get_barrier_semaphore()

    def greet(step, _):
        peer = place_of((me + step) % devices)
        pl.semaphore_signal(
            barrier, inc=1, device_id=peer, device_id_type=pl.DeviceIdType.MESH
        )
        return 0

    lax.fori_loop(1, devices, greet, 0)

    def encode(part, _):
        here = pl.ds(part * (QTILE // BLOCK), QTILE // BLOCK)
        linear = jnp.dot(
            summed_ref[here].reshape(QTILE, -1), cpe_ref[...], preferred_element_type=jnp.float32
        )
        own = own_ref[here].reshape(QTILE, -1).astype(jnp.float32)
        encoded = (own + normalised(linear, cpe_gain_ref[...])).astype(jnp.bfloat16)
        outgoing_ref[here] = encoded.reshape(QTILE // BLOCK, BLOCK, -1)
        return 0

    lax.fori_loop(0, devices * BLOCK // QTILE, encode, 0, unroll=4)
    pl.semaphore_wait(barrier, devices - 1)

    def send(step, _):
        peer = (me + step) % devices
        to_peer(notes_ref.at[peer], heard_ref.at[me], note_sems, peer).start()
        to_peer(outgoing_ref.at[peer], arrived_ref.at[me], block_sems, peer).start()
        return 0

    lax.fori_loop(1, devices, send, 0)
    arrived_ref[me] = outgoing_ref[me]
    heard_ref[me] = notes_ref[me]
    others = pl.ds(0, devices - 1)
    all_notes = to_peer(notes_ref.at[others], heard_ref.at[others], note_sems, me)
    all_notes.wait_recv()

    heard = heard_ref[...].reshape(devices, LANES)
    source = lax.broadcasted_iota(jnp.int32, (devices, LANES), 0)
    lane = lax.broadcasted_iota(jnp.int32, (devices, LANES), 1)
    slots = heard[:, :1]
    index_ref[...] = jnp.max(jnp.where(slots == lane, source, 0), axis=0, keepdims=True)
    counts = heard[:, 1:2]
    offset = jnp.sum(jnp.where(source < me, counts, 0), axis=0, keepdims=True)
    rest = jnp.sum(jnp.where(source < me, 0, counts), axis=0, keepdims=True)
    summary_ref[...] = jnp.where(lane[:1] == 0, offset, rest)
    order = pltpu.make_async_copy(index_ref, order_ref, local_sem)
    order.start()
    order.wait()

    all_blocks = to_peer(outgoing_ref.at[others], arrived_ref.at[others], block_sems, me)
    all_blocks.wait_recv()

    def settle(slot, _):
        block = arrived_ref[order_ref[0, slot]]
        row = pl.multiple_of(slot * BLOCK, BLOCK)
        moved_ref[pl.ds(row, BLOCK), :] = block
        put(wide_ref, row, block.astype(jnp.float32))
        return 0

    lax.fori_loop(0, devices, settle, 0, unroll=8)
    following = (me + 1) % devices
    previous = (me + devices - 1) % devices
    head_sems = (side_send_sem.at[0], side_recv_sem.at[0])
    tail_sems = (side_send_sem.at[1], side_recv_sem.at[1])
    rows = devices * BLOCK
    head = to_peer(normed_ref.at[pl.ds(0, PATCH)], after_ref, head_sems, previous)
    tail = to_peer(tail_ref, before_ref, tail_sems, following)
    start = jnp.clip(count_ref[0] - PATCH, 0, rows - PATCH)

    def first_norm(first):
        return normalised(get(wide_ref, first, QTILE), gain_ref[...]).astype(jnp.bfloat16)

    for part in range(PATCH // QTILE):
        here = pl.ds(part * QTILE, QTILE)
        tail_ref[here, :] = first_norm(start + part * QTILE)
        to_peer(tail_ref.at[here], before_ref.at[here], tail_sems, following).start()
        normed_ref[here, :] = first_norm(part * QTILE)
        to_peer(normed_ref.at[here], after_ref.at[here], head_sems, previous).start()
    for part in range(PATCH // QTILE, rows // QTILE):
        normed_ref[pl.ds(part * QTILE, QTILE), :] = first_norm(part * QTILE)
    all_notes.wait_send()
    all_blocks.wait_send()
    head.wait()
    tail.wait()


def exchanged(count, summed, own, notes, cpe_weight, cpe_gain, gain):
    blocks, block, width = summed.shape
    rows = blocks * block
    vmem = pl.BlockSpec(memory_space=pltpu.VMEM)
    smem = pl.BlockSpec(memory_space=pltpu.SMEM)
    whole = jax.ShapeDtypeStruct((rows, width), jnp.bfloat16)
    side = jax.ShapeDtypeStruct((PATCH, width), jnp.bfloat16)
    dma = pltpu.SemaphoreType.DMA
    return pl.pallas_call(
        exchange_kernel,
        out_shape=(
            whole,
            whole,
            side,
            side,
            jax.ShapeDtypeStruct((1, LANES), jnp.int32),
        ),
        in_specs=[smem] + [vmem] * 6,
        out_specs=(vmem,) * 5,
        scratch_shapes=[
            pltpu.VMEM((blocks, block, width), jnp.bfloat16),
            pltpu.VMEM((blocks, block, width), jnp.bfloat16),
            pltpu.VMEM((blocks, 1, LANES), jnp.int32),
            pltpu.VMEM((width // LANES, rows, LANES), jnp.float32),
            pltpu.VMEM((PATCH, width), jnp.bfloat16),
            pltpu.VMEM((1, LANES), jnp.int32),
            pltpu.SMEM((1, LANES), jnp.int32),
            dma,
            dma,
            dma,
            dma,
            dma((2,)),
            dma((2,)),
            dma,
        ],
        compiler_params=pltpu.CompilerParams(
            vmem_limit_bytes=32 << 20, has_side_effects=True, collective_id=0
        ),
        name="exchange",
    )(count, summed, own, notes, cpe_weight, cpe_gain, gain)


def block_kernel(
    summary_ref,
    count_ref,
    moved_ref,
    normed_ref,
    tail_ref,
    head_ref,
    qkv_ref,
    proj_ref,
    gain_two_ref,
    fc_one_ref,
    fc_two_ref,
    out_ref,
    source_ref,
    own_ref,
    keys_ref,
    values_ref,
    result_ref,
    gathered_ref,
    reach_ref,
    size_ref,
):
    rows, width = moved_ref.shape
    skew = summary_ref[0, 0] % PATCH
    live = count_ref[0]
    known = summary_ref[0, 1] + skew
    live_end = skew + live

    for part in range(PATCH // QTILE):
        piece = tail_ref[part * QTILE : (part + 1) * QTILE, :].astype(jnp.float32)
        put(source_ref, skew + part * QTILE, piece)
    for part in range(rows // QTILE):
        piece = moved_ref[part * QTILE : (part + 1) * QTILE, :].astype(jnp.float32)
        put(own_ref, skew + part * QTILE, piece)
        piece = normed_ref[part * QTILE : (part + 1) * QTILE, :].astype(jnp.float32)
        put(source_ref, PATCH + skew + part * QTILE, piece)
    for part in range(PATCH // QTILE):
        piece = head_ref[part * QTILE : (part + 1) * QTILE, :].astype(jnp.float32)
        put(source_ref, PATCH + live_end + part * QTILE, piece)

    head_of_lane = lax.broadcasted_iota(jnp.int32, (QTILE, width), 1) // (width // HEADS)
    left = lax.broadcasted_iota(jnp.int32, (width, width), 0) // (width // HEADS)
    right = lax.broadcasted_iota(jnp.int32, (width, width), 1) // (width // HEADS)
    same_head = jnp.where(left == right, 1.0, 0.0).astype(jnp.bfloat16)

    def squares(values):
        values = values.astype(jnp.float32)
        total = jnp.dot(
            (values * values).astype(jnp.bfloat16), same_head, preferred_element_type=jnp.float32
        )
        return 1.02 * total

    per_patch = PATCH // QTILE
    patches = (live_end + PATCH - 1) // PATCH

    @pl.loop(0, patches)
    def _(patch):
        for part in range(per_patch):
            start = pl.multiple_of(PATCH + patch * PATCH + part * QTILE, QTILE)
            pair = jnp.dot(
                get(source_ref, start, QTILE).astype(jnp.bfloat16),
                qkv_ref[:, width:],
                preferred_element_type=jnp.float32,
            )
            columns = slice(part * QTILE, (part + 1) * QTILE)
            some_keys = pair[:, :width].astype(jnp.bfloat16).astype(jnp.float32)
            keys_ref[patch, :, columns] = some_keys.T.astype(jnp.bfloat16)
            alive = start - PATCH + lax.broadcasted_iota(jnp.int32, (QTILE, 1), 0) < known
            some_values = pair[:, width:].astype(jnp.bfloat16)
            for odd in range(2):
                fitted = jnp.where(head_of_lane % 2 == odd, some_values, jnp.bfloat16(1))
                values_ref[patch, odd, columns, :] = jnp.where(alive, fitted, jnp.bfloat16(0))
            reach = jnp.max(squares(some_keys), axis=0, keepdims=True)
            size = jnp.max(jnp.abs(pair[:, width:]), axis=0, keepdims=True)
            reach_ref[patch] = reach if part == 0 else jnp.maximum(reach_ref[patch], reach)
            size_ref[patch] = size if part == 0 else jnp.maximum(size_ref[patch], size)


    def finish(start):
        spots = start + lax.broadcasted_iota(jnp.int32, (QTILE, 1), 0)
        attended = jnp.where(spots < live_end, gathered_ref[...], 0.0)
        projected = jnp.dot(
            attended.astype(jnp.bfloat16), proj_ref[...], preferred_element_type=jnp.float32
        )
        mixed = (get(own_ref, start, QTILE) + projected).astype(jnp.bfloat16).astype(jnp.float32)
        normed = normalised(mixed, gain_two_ref[...]).astype(jnp.bfloat16)
        hidden = jnp.dot(normed, fc_one_ref[...], preferred_element_type=jnp.float32)
        hidden = 0.5 * hidden * (1.0 + lax.erf(hidden * 0.5**0.5))
        final = mixed + jnp.dot(
            hidden.astype(jnp.bfloat16), fc_two_ref[...], preferred_element_type=jnp.float32
        )
        put(result_ref, start, final)

    first_tile = skew // QTILE
    live_tiles = (live_end + QTILE - 1) // QTILE
    all_tiles = (skew + rows + QTILE - 1) // QTILE

    @pl.loop(first_tile, live_tiles)
    def _(tile):
        start = pl.multiple_of(tile * QTILE, QTILE)
        before = pl.multiple_of(jnp.maximum(tile - 1, 0) * QTILE, QTILE)
        patch = tile // per_patch
        normed = get(source_ref, pl.multiple_of(PATCH + start, QTILE), QTILE).astype(jnp.bfloat16)
        queries = jnp.dot(normed, qkv_ref[:, :width], preferred_element_type=jnp.float32)
        queries = queries.astype(jnp.bfloat16) * jnp.bfloat16((width // HEADS) ** -0.5)
        reach = jnp.max(squares(queries) * reach_ref[patch])
        safe = (reach <= SAFE_SCORE**2) & (jnp.max(size_ref[patch]) <= SAFE_VALUE)

        def grow(group, odd, softened):
            heads = [2 * (group * STACK + index) + odd for index in range(STACK)]
            one = jnp.concatenate(
                [jnp.where(head_of_lane == head, queries, jnp.bfloat16(0)) for head in heads],
                axis=0,
            )
            scores = jnp.dot(one, keys_ref[patch], preferred_element_type=jnp.float32)
            return heads, softened(scores).astype(jnp.bfloat16)

        def gather(heads, odd, grown, so_far):
            mixed = jnp.dot(grown, values_ref[patch, odd], preferred_element_type=jnp.float32)
            spare = LANES - 1 if odd == 0 else 0
            mixed = mixed * (1.0 / mixed[:, spare : spare + 1])
            for index, head in enumerate(heads):
                piece = mixed[index * QTILE : (index + 1) * QTILE]
                so_far = jnp.where(head_of_lane == head, piece, so_far)
            return so_far

        @pl.when(safe)
        def _():
            steps = [(group, odd) for group in range(HEADS // (2 * STACK)) for odd in range(2)]
            so_far = jnp.zeros((QTILE, width), jnp.float32)
            ready = [grow(*steps[0], jnp.exp)]
            finish(before)
            for index, (_, odd) in enumerate(steps):
                if index + 1 < len(steps):
                    ready.append(grow(*steps[index + 1], jnp.exp))
                so_far = gather(ready[index][0], odd, ready[index][1], so_far)
            gathered_ref[...] = so_far

        @pl.when(jnp.logical_not(safe))
        def _():
            finish(before)
            spot = patch * PATCH + lax.broadcasted_iota(jnp.int32, (1, PATCH), 1)
            bias = jnp.where(spot < known, 0.0, -1e30)

            def softened(scores):
                scores = scores + bias
                return jnp.exp(scores - jnp.max(scores, axis=-1, keepdims=True))

            @pl.loop(0, HEADS // (2 * STACK))
            def _(group):
                for odd in range(2):
                    heads, grown = grow(group, odd, softened)
                    gathered_ref[...] = gather(heads, odd, grown, gathered_ref[...])

    @pl.loop(live_tiles - 1, all_tiles)
    def _(tile):
        finish(pl.multiple_of(tile * QTILE, QTILE))
        gathered_ref[...] = jnp.zeros((QTILE, width), jnp.float32)

    for part in range(rows // QTILE):
        out_ref[part * QTILE : (part + 1) * QTILE, :] = get(
            result_ref, skew + part * QTILE, QTILE
        ).astype(jnp.bfloat16)


def finished(summary, count, moved, normed, tail, head, qkv, proj, gain_two, fc_one, fc_two):
    rows, width = moved.shape
    vmem = pl.BlockSpec(memory_space=pltpu.VMEM)
    smem = pl.BlockSpec(memory_space=pltpu.SMEM)
    most = rows // PATCH + 1
    halves = width // LANES
    return pl.pallas_call(
        block_kernel,
        out_shape=jax.ShapeDtypeStruct((rows, width), jnp.bfloat16),
        in_specs=[smem, smem] + [vmem] * 9,
        out_specs=vmem,
        scratch_shapes=[
            pltpu.VMEM((halves, (most + 2) * PATCH, LANES), jnp.float32),
            pltpu.VMEM((halves, most * PATCH, LANES), jnp.float32),
            pltpu.VMEM((most, width, PATCH), jnp.bfloat16),
            pltpu.VMEM((most, 2, PATCH, width), jnp.bfloat16),
            pltpu.VMEM((halves, most * PATCH, LANES), jnp.float32),
            pltpu.VMEM((QTILE, width), jnp.float32),
            pltpu.VMEM((most, 1, width), jnp.float32),
            pltpu.VMEM((most, 1, width), jnp.float32),
        ],
        compiler_params=pltpu.CompilerParams(vmem_limit_bytes=36 << 20),
        name="attend",
    )(summary, count, moved, normed, tail, head, qkv, proj, gain_two, fc_one, fc_two)


def per_device(
    features,
    neighbours,
    counts,
    block_dest,
    conv_weight,
    cpe_weight,
    cpe_gain,
    norm1_gain,
    qkv_weight,
    proj_weight,
    norm2_gain,
    fc1_weight,
    fc2_weight,
):
    rows, width = features.shape[2:]
    taps = neighbours.shape[2]
    def afar(value):
        return pltpu.with_memory_space_constraint(value, pltpu.HBM)

    own_count = counts.reshape(1)
    summed, own, notes = convolved(
        afar(features.reshape(rows, width)),
        afar(neighbours.reshape(taps, rows // TILE, TILE)),
        afar(block_dest.reshape(-1)),
        own_count,
        afar(conv_weight.reshape(taps * width, width)),
    )
    moved, normed, before, after, summary = exchanged(
        own_count,
        summed,
        own,
        notes,
        cpe_weight,
        cpe_gain.reshape(1, width),
        norm1_gain.reshape(1, width),
    )
    block_out = finished(
        summary,
        own_count,
        moved,
        normed,
        before,
        after,
        qkv_weight,
        proj_weight,
        norm2_gain.reshape(1, width),
        fc1_weight,
        fc2_weight,
    )
    return block_out.reshape(1, 1, rows, width)


def solution(mesh):
    placed = (
        P("gx", "gy", None, None),
        P("gx", "gy", None, None),
        P("gx", "gy"),
        P("gx", "gy", None),
    ) + (P(),) * 9
    return jax.shard_map(
        per_device, mesh=mesh, in_specs=placed, out_specs=P("gx", "gy", None, None), check_vma=False
    )
```
